256 devices in a mesh: tile: 4 (over z_lo, core), freq: 64 (over y, z_hi, x).
Axes of the slice: x: 4, y: 4, z: 8 (z_hi: 4, z_lo: 2; z = z_hi * 2 + z_lo), core: 2. Of those that a mesh axis runs over, the one named last changes fastest.
Arguments:
- sky: bfloat16 [4, 512, 2, 4096], P('tile', 'freq'), may hold values from -6 to 6
- kernel: bfloat16 [4, 64, 2, 4096, 128], P('tile', 'freq'), may hold values from -0.0625 to 0.0625
- data: bfloat16 [64, 2, 128, 512], P('freq'), may hold values from -6 to 6
- block_tiles: int32 [64, 4], P('freq'), may hold values 0 or 1
- length_bin: int32 [64, 128], P('freq'), may hold values from 0 to 31
- wedge_keep: int32 [32, 512], replicated, may hold values 0 or 1
Outputs:
- gradient: float32 [4, 512, 2, 4096], P('tile', 'freq')
The draws below stay inside these ranges and needn't reach their ends.
All inputs are finite; a program needn't handle non-finite values. No bound on the sum of `block_tiles` on one device may be relied on, other than what follows from the above.
Results may differ from the reference program's by a relative error of at most 0.0027.
Values may be sent and summed in bfloat16 or wider, within the bound.
A program may use at most 128 MiB of HBM per device.

```python
import math
import jax
import jax.numpy as jnp
from jax import lax

CELLS = 4096
CH = 512
BL = 128
LBINS = 32
NBLK = 64
TILES = 4


def with_ends(entries, own_key, low, top_value):
    spot = [jax.random.randint(jax.random.fold_in(own_key, axis), (), 0, length) for axis, length in enumerate(entries.shape)]
    main_axis = entries.shape.index(max(entries.shape))
    neighbour = spot[:main_axis] + [(spot[main_axis] + 1) % entries.shape[main_axis]] + spot[main_axis + 1:]
    return entries.at[tuple(spot)].set(low).at[tuple(neighbour)].set(top_value)


def block_scale(own_key, shape, split, least, top_value):
    factor_of = 1.0
    for axis_at, shards_of in split:
        heights = jax.random.uniform(jax.random.fold_in(jax.random.fold_in(own_key, 6), axis_at), (shards_of,), jnp.float32, least / len(split), top_value / len(split))
        factor_of = factor_of * jnp.repeat(jnp.exp(heights), shape[axis_at] // shards_of).reshape((-1,) + (1,) * (len(shape) - 1 - axis_at))
    return factor_of


def bell_draw(stream_key, shape, deviation, limit, split=(), held_as=jnp.bfloat16):
    array = deviation * jax.random.normal(stream_key, shape, jnp.float32)
    if split:
        array = array * block_scale(stream_key, shape, split, -0.22, 0.18)
    return jnp.clip(array, -limit, limit).astype(held_as)


def setup_inputs(seed: int = 0) -> dict:
    arg_keys = jax.random.split(jax.random.key(seed), 7)
    return {
        "sky": bell_draw(arg_keys[0], (TILES, CH, 2, CELLS), 1.0, 6.0, ((0, 4), (1, 64))),
        "kernel": bell_draw(arg_keys[1], (TILES, NBLK, 2, CELLS, BL), (2 * CELLS) ** -0.5, 0.0625, ((0, 4), (1, 64))),
        "data": bell_draw(arg_keys[2], (NBLK, 2, BL, CH), 1.0, 6.0, ((0, 64),)),
        "block_tiles": with_ends((jax.random.randint(arg_keys[3], (NBLK, TILES), 0, 4) < 3).astype(jnp.int32), jax.random.fold_in(arg_keys[3], 1), 0, 1),
        "length_bin": with_ends(jax.random.randint(arg_keys[4], (NBLK, BL), 0, LBINS), jax.random.fold_in(arg_keys[4], 1), 0, LBINS - 1).astype(jnp.int32),
        "wedge_keep": with_ends((jax.random.randint(arg_keys[5], (LBINS, CH), 0, 2) < 1).astype(jnp.int32), jax.random.fold_in(arg_keys[5], 1), 0, 1),
    }


def delay_tables(length):
    indices = jnp.arange(length, dtype=jnp.int32)
    product = indices[:, None] * indices[None, :] % length
    angle = product.astype(jnp.float32) * (2.0 * math.pi / length)
    return (jnp.cos(angle), jnp.sin(angle))

def real_form(kernel_pair):
    upper_half = jnp.concatenate([kernel_pair[0], kernel_pair[1]], axis=1)
    lower_half = jnp.concatenate([-kernel_pair[1], kernel_pair[0]], axis=1)
    return jnp.concatenate([upper_half, lower_half], axis=0)

def transform(values, table):
    return jnp.einsum('...c,ck->...k', values, table, precision=lax.Precision.HIGHEST)

def back_project(visibility, data, keep_mask, cosine, sine_table):
    norm_factor = 1.0 / math.sqrt(cosine.shape[0])
    real_vis = visibility[:, 0]
    imag_vis = visibility[:, 1]
    spec_real = (transform(real_vis, cosine) + transform(imag_vis, sine_table)) * norm_factor
    spec_imag = (transform(imag_vis, cosine) - transform(real_vis, sine_table)) * norm_factor
    miss_real = keep_mask * (spec_real - data[:, 0].astype(jnp.float32))
    miss_imag = keep_mask * (spec_imag - data[:, 1].astype(jnp.float32))
    back_real = (transform(miss_real, cosine) - transform(miss_imag, sine_table)) * norm_factor
    back_imag = (transform(miss_imag, cosine) + transform(miss_real, sine_table)) * norm_factor
    return jnp.stack([back_real, back_imag], axis=1).astype(jnp.bfloat16)

def reference(sky, kernel, data, block_tiles, length_bin, wedge_keep):
    cosine, sine_table = delay_tables(CH)
    flat_sky = sky.reshape(TILES, CH, 2 * CELLS)

    def forward(block):
        running = jnp.zeros((CH, 2 * BL), jnp.float32)
        for tile_num in range(TILES):
            weight = block_tiles[block, tile_num].astype(jnp.float32)
            running = running + weight * jnp.dot(flat_sky[tile_num], real_form(kernel[tile_num, block]), preferred_element_type=jnp.float32)
        return running.T.reshape(2, BL, CH)
    visibility = lax.map(forward, jnp.arange(NBLK, dtype=jnp.int32))
    keep_mask = wedge_keep[length_bin].astype(jnp.float32)
    back_field = back_project(visibility, data, keep_mask, cosine, sine_table)

    def adjoint(running, block):
        field_rows = back_field[block].reshape(2 * BL, CH)
        updates = []
        for tile_num in range(TILES):
            weight = block_tiles[block, tile_num].astype(jnp.float32)
            updates.append(weight * jnp.dot(field_rows.T, real_form(kernel[tile_num, block]).T, preferred_element_type=jnp.float32))
        return (running + jnp.stack(updates), None)
    start_grad = jnp.zeros((TILES, CH, 2 * CELLS), jnp.float32)
    gradient, _ = lax.scan(adjoint, start_grad, jnp.arange(NBLK, dtype=jnp.int32))
    return gradient.reshape(TILES, CH, 2, CELLS)
```

```python
import functools
import math

import jax
import jax.numpy as jnp
import numpy as np
from jax import lax
from jax.experimental import pallas as pl
from jax.experimental.pallas import tpu as pltpu
from jax.sharding import Mesh
from jax.sharding import PartitionSpec as P

FREQ = ("freq_0", "freq_1", "freq_2")
AXES = ("tile",) + FREQ
RING = 4
ROWS = 16
GATHER_PLANES = (0, 1, 3, 2)
REDUCE_PLANES = (2, 1, 3, 0)


def at(dx, dy):
    return (dx % RING) * RING + dy % RING


def forward_class(dz, other):
    return 1 if (dz + other) % 2 == 0 else -1


def gather_keys():
    keys = [(dz, 0, "F") for dz in range(1, RING)]
    for dz in range(RING):
        for d in range(1, RING):
            keys += [(dz, at(d, 0), "F"), (dz, at(0, d), "F")]
        for dx in range(1, RING):
            for dy in range(1, RING):
                keys += [(dz, at(dx, dy), "A"), (dz, at(dx, dy), "B")]
    return {key: n for n, key in enumerate(keys)}


GATHER = gather_keys()


def reduce_slots():
    halves, fulls = [], []
    for dz in range(RING):
        for d in range(1, RING):
            for came in (1, -1):
                halves.append((dz, at(d, 0), "A", "y", came))
                halves.append((dz, at(0, d), "B", "x", came))
            side = forward_class(dz, d)
            halves.append((dz, at(d, -side), "A", "y", side))
            halves.append((dz, at(-side, d), "B", "x", side))
        side = forward_class(dz, 0)
        fulls.append((dz, at(-side, 0), "F", "x", side))
        fulls.append((dz, at(0, -side), "F", "y", side))
        for axis in "xy":
            for came in (1, -1):
                fulls.append((dz, 0, "F", axis, came))
    return {k: n for n, k in enumerate(halves)}, {k: n for n, k in enumerate(fulls)}


HALVES, FULLS = reduce_slots()


def kernel(
    bt_ref, sky_ref, ker_ref, data_ref, bins_ref, wedge_ref, thi_ref, tlo_ref, out_ref,
    buf, kc, acc, vp, t1r, hs, hr, vis, spec, vhi, vlo, mask, dat, u, g,
    rs_h, rs_f, zs, zr,
    local_sem, send_sem, ag_sem, t_send, t_recv, rh_sem, rf_sem, z_send, z_recv,
):
    tile = lax.axis_index("tile")
    y = lax.axis_index("freq_0")
    z = lax.axis_index("freq_1")
    x = lax.axis_index("freq_2")
    cells = sky_ref.shape[1]
    half = cells // 2
    chans, base = vis.shape[1], vis.shape[2]
    per = chans // RING**3
    core = lax.rem(tile, 2)
    mate = tile + 1 - 2 * core

    def near(axis, step):
        if axis == "x":
            return (tile, y, z, lax.rem(x + step + RING, RING))
        if axis == "y":
            return (tile, lax.rem(y + step + RING, RING), z, x)
        return (tile, y, lax.rem(z + step + RING, RING), x)

    over = lax.rem(tile + 2, 4)
    cross = lax.rem(mate + 2, 4)
    peers = [near("x", 1), near("x", -1), near("y", 1), near("y", -1)]
    peers += [near("z", d) for d in (1, 2, 3)]
    peers += [(t, y, z, x) for t in (mate, over, cross)]

    load_sky = pltpu.make_async_copy(sky_ref, buf.at[0, 0], local_sem.at[0])
    load_r = pltpu.make_async_copy(ker_ref.at[0], kc.at[:, 0:base], local_sem.at[1])
    load_i = pltpu.make_async_copy(ker_ref.at[1], kc.at[:, base : 2 * base], local_sem.at[2])
    load_sky.start()
    load_r.start()
    load_i.start()
    barrier = pltpu.get_barrier_semaphore()
    for peer in peers:
        pl.semaphore_signal(barrier, inc=1, device_id=peer, device_id_type=pl.DeviceIdType.MESH)
    pl.semaphore_wait(barrier, len(peers))

    def part_of(ref, dz, cell, part):
        if part == "F":
            return ref.at[dz, cell]
        lo = 0 if part == "A" else half
        return ref.at[dz, cell, :, lo : lo + half]

    def remote(src, dst, send, recv, peer):
        return pltpu.make_async_remote_copy(
            src_ref=src, dst_ref=dst, send_sem=send, recv_sem=recv,
            device_id=peer, device_id_type=pl.DeviceIdType.MESH,
        )

    weight = bt_ref[0, tile].astype(jnp.float32)

    sent = []

    def gather_send(dz, dx, dy, part, axis, step):
        if axis == "z":
            new = ((dz - step) % RING, 0)
        else:
            new = (dz, at(dx - step, dy) if axis == "x" else at(dx, dy - step))
        copy = remote(
            part_of(buf, dz, at(dx, dy), part),
            part_of(buf, *new, part),
            send_sem.at[len(sent)],
            ag_sem.at[GATHER[(*new, part)]],
            near(axis, step),
        )
        copy.start()
        sent.append(copy)

    def gather_wait(dz, dx, dy, part):
        ref = part_of(buf, dz, at(dx, dy), part)
        remote(ref, ref, send_sem.at[0], ag_sem.at[GATHER[(dz, at(dx, dy), part)]],
               near("x", 1)).wait_recv()

    def g1(dz):
        if dz:
            gather_wait(dz, 0, 0, "F")
        for axis in "xy":
            for step in (1, -1):
                gather_send(dz, 0, 0, "F", axis, step)

    def g2(dz):
        side = forward_class(dz, 0)
        for d in (-side, side):
            for axis, turn, part in (("x", "y", "A"), ("y", "x", "B")):
                dx, dy = (d, 0) if axis == "x" else (0, d)
                gather_wait(dz, dx, dy, "F")
                if d == -side:
                    gather_send(dz, dx, dy, "F", axis, side)
                for step in (1, -1):
                    gather_send(dz, dx, dy, part, turn, step)

    def g3(dz):
        for turn, part, dx, dy in (("y", "A", 2, 0), ("x", "B", 0, 2)):
            gather_wait(dz, dx, dy, "F")
            for step in (1, -1):
                gather_send(dz, dx, dy, part, turn, step)

    def g4(dz):
        for d in (1, 3, 2):
            side = forward_class(dz, d)
            for far in (-side, side):
                gather_wait(dz, d, far, "A")
                if far == -side:
                    gather_send(dz, d, far, "A", "y", side)
                gather_wait(dz, far, d, "B")
                if far == -side:
                    gather_send(dz, far, d, "B", "x", side)

    def g5(dz):
        for d in (1, 3, 2):
            gather_wait(dz, d, 2, "A")
            gather_wait(dz, 2, d, "B")

    depth = 512
    deep = cells // depth

    def forward(dz):
        acc[...] = jnp.zeros_like(acc)

        @pl.loop(0, deep)
        def _(k):
            lanes = pl.ds(pl.multiple_of(k * depth, depth), depth)
            rows = buf[dz, :, :, lanes].reshape(RING * RING * ROWS, depth)
            acc[...] += jnp.dot(rows, kc[lanes, :], preferred_element_type=jnp.float32)

        out = acc[...].reshape(RING * RING, 2, per, 2 * base)
        real = out[:, 0, :, :base] - out[:, 1, :, base:]
        imag = out[:, 1, :, :base] + out[:, 0, :, base:]
        vp[dz, 0] = (real * weight).reshape(RING * RING * per, base)
        vp[dz, 1] = (imag * weight).reshape(RING * RING * per, base)

    def t1(dz):
        return remote(vp.at[dz, 1 - core], t1r.at[dz], t_send.at[dz, 0], t_recv.at[dz, 0],
                      (mate, y, z, x))

    def t2(dz):
        return [
            remote(hs.at[dz], hr.at[dz, n], t_send.at[dz, n + 1], t_recv.at[dz, n + 1],
                   (t, y, z, x))
            for n, t in enumerate((mate, over, cross))
        ]

    def tile_first(dz):
        forward(dz)
        t1(dz).start()

    def tile_second(dz):
        t1(dz).wait_recv()
        hs[dz] = vp[dz, core] + t1r[dz]
        for copy in t2(dz):
            copy.start()

    def row_of(dz, cell):
        sx = lax.rem(x + cell // RING, RING)
        sy = lax.rem(y + cell % RING, RING)
        sz = lax.rem(z + dz, RING)
        return pl.multiple_of((sy * RING * RING + sz * RING + sx) * per, per)

    def tile_third(dz):
        for copy in t2(dz):
            copy.wait_recv()
        for cell in range(RING * RING):
            mine = pl.ds(cell * per, per)
            rows = pl.ds(row_of(dz, cell), per)
            vis[core, rows, :] = hs[dz, mine, :] + hr[dz, 1, mine, :]
            vis[1 - core, rows, :] = hr[dz, 0, mine, :] + hr[dz, 2, mine, :]

    def prepare():
        levels = lax.broadcasted_iota(jnp.int32, (wedge_ref.shape[0], base), 0)
        hot = (levels == bins_ref[...]).astype(jnp.bfloat16)
        keep = wedge_ref[...].astype(jnp.float32).T.astype(jnp.bfloat16)
        mask[...] = jnp.dot(keep, hot, preferred_element_type=jnp.float32)
        for plane in range(2):
            dat[plane] = data_ref[plane].astype(jnp.float32).T

    load_sky.wait()
    for step in (1, 3, 2):
        gather_send(0, 0, 0, "F", "z", step)
    p = GATHER_PLANES
    g1(p[0])
    prepare()
    g1(p[1])
    g2(p[0])
    g3(p[0])
    load_r.wait()
    load_i.wait()
    g1(p[2])
    g2(p[1])
    g4(p[0])
    g3(p[1])
    g1(p[3])
    g2(p[2])
    g5(p[0])
    tile_first(p[0])
    g4(p[1])
    g3(p[2])
    g2(p[3])
    tile_second(p[0])
    g5(p[1])
    tile_first(p[1])
    g4(p[2])
    g3(p[3])
    tile_second(p[1])
    tile_third(p[0])
    g5(p[2])
    tile_first(p[2])
    g4(p[3])
    tile_second(p[2])
    tile_third(p[1])
    g5(p[3])
    tile_first(p[3])
    tile_third(p[2])
    tile_second(p[3])
    for copy in sent:
        copy.wait_send()
    tile_third(p[3])
    for dz in range(RING):
        for copy in (t1(dz), *t2(dz)):
            copy.wait_send()

    norm = 1.0 / math.sqrt(chans)
    block = 256

    def transform():
        for plane in range(2):
            lanes = slice(plane * base, (plane + 1) * base)
            whole = vis[plane]
            vhi[:, lanes] = whole.astype(jnp.bfloat16)
            vlo[:, lanes] = (whole - vhi[:, lanes].astype(jnp.float32)).astype(jnp.bfloat16)

        @pl.loop(0, 2 * chans // block)
        def _(n):
            rows = pl.ds(pl.multiple_of(n * block, block), block)
            spec[rows, :] = (
                jnp.dot(thi_ref[rows, :], vhi[...], preferred_element_type=jnp.float32)
                + jnp.dot(thi_ref[rows, :], vlo[...], preferred_element_type=jnp.float32)
                + jnp.dot(tlo_ref[rows, :], vhi[...], preferred_element_type=jnp.float32)
            )

    cos_rows, sin_rows = slice(0, chans), slice(chans, 2 * chans)
    lane_r, lane_i = slice(0, base), slice(base, 2 * base)
    transform()
    vis[0] = mask[...] * (
        (spec[cos_rows, lane_r] + spec[sin_rows, lane_i]) * norm - dat[0]
    )
    vis[1] = mask[...] * (
        (spec[cos_rows, lane_i] - spec[sin_rows, lane_r]) * norm - dat[1]
    )
    transform()
    vis[0] = (spec[cos_rows, lane_r] - spec[sin_rows, lane_i]) * (norm * weight)
    vis[1] = (spec[cos_rows, lane_i] + spec[sin_rows, lane_r]) * (norm * weight)
    for dz in range(RING):
        for cell in range(RING * RING):
            rows = pl.ds(row_of(dz, cell), per)
            ur, ui = vis[0, rows, :], vis[1, rows, :]
            top = jnp.concatenate([ur, ui], axis=1)
            low = jnp.concatenate([ui, -ur], axis=1)
            u[dz, cell] = jnp.concatenate([top, low], axis=0).astype(jnp.bfloat16)

    def backward(dz):
        rows = u[dz].reshape(RING * RING * ROWS, 2 * base)

        @pl.loop(0, deep)
        def _(k):
            lanes = pl.ds(pl.multiple_of(k * depth, depth), depth)
            part = lax.dot_general(
                rows, kc[lanes, :], (((1,), (1,)), ((), ())),
                preferred_element_type=jnp.float32,
            )
            g[dz, :, :, lanes] = part.reshape(RING * RING, ROWS, depth)

    back_sent = []

    def slot(dz, cell, part, axis, came):
        key = (dz, cell, part, axis, came)
        if part == "F":
            return rs_f.at[FULLS[key]], rf_sem.at[FULLS[key]]
        return rs_h.at[HALVES[key]], rh_sem.at[HALVES[key]]

    def reduce_send(dz, dx, dy, part, axis, step):
        new = at(dx - step, dy) if axis == "x" else at(dx, dy - step)
        dst, sem = slot(dz, new, part, axis, -step)
        copy = remote(
            part_of(buf, dz, at(dx, dy), part), dst, send_sem.at[len(back_sent)], sem,
            near(axis, step),
        )
        copy.start()
        back_sent.append(copy)

    def arrived(dz, dx, dy, part, axis, came):
        ref, sem = slot(dz, at(dx, dy), part, axis, came)
        remote(ref, ref, send_sem.at[0], sem, near("x", 1)).wait_recv()
        return ref, part

    width = 1024

    def total(dst, dz, dx, dy, part, terms):
        cell = at(dx, dy)
        start = half if part == "B" else 0
        stop = half if part == "A" else cells

        def step_of(n):
            lanes = pl.ds(pl.multiple_of(start + n * width, width), width)
            value = g[dz, cell, :, lanes]
            for ref, kind in terms:
                shift = half if kind == "B" else 0
                own = pl.ds(pl.multiple_of(start - shift + n * width, width), width)
                value = value + ref[:, own].astype(jnp.float32)
            dst[:, lanes] = value.astype(dst.dtype)

        pl.loop(0, (stop - start) // width)(step_of)

    def r1(dz):
        backward(dz)
        for d in (2, 1, 3):
            side = forward_class(dz, d)
            total(buf.at[dz, at(d, 2)], dz, d, 2, "A", [])
            reduce_send(dz, d, 2, "A", "y", -side)
            total(buf.at[dz, at(2, d)], dz, 2, d, "B", [])
            reduce_send(dz, 2, d, "B", "x", -side)
            total(buf.at[dz, at(d, side)], dz, d, side, "A", [])
            reduce_send(dz, d, side, "A", "y", side)
            total(buf.at[dz, at(side, d)], dz, side, d, "B", [])
            reduce_send(dz, side, d, "B", "x", side)

    def r2(dz):
        for d in (2, 1, 3):
            side = forward_class(dz, d)
            got = arrived(dz, d, -side, "A", "y", side)
            total(buf.at[dz, at(d, -side)], dz, d, -side, "A", [got])
            reduce_send(dz, d, -side, "A", "y", -side)
            got = arrived(dz, -side, d, "B", "x", side)
            total(buf.at[dz, at(-side, d)], dz, -side, d, "B", [got])
            reduce_send(dz, -side, d, "B", "x", -side)

    def on_axis(dz, axis, d, fulls):
        dx, dy = (d, 0) if axis == "x" else (0, d)
        turn, part, rest = ("y", "A", "B") if axis == "x" else ("x", "B", "A")
        got = [arrived(dz, dx, dy, part, turn, came) for came in (1, -1)]
        dst = buf.at[dz, at(dx, dy)]
        total(dst, dz, dx, dy, part, got + fulls)
        total(dst, dz, dx, dy, rest, fulls)

    def r3(dz):
        side = forward_class(dz, 0)
        for axis in "xy":
            dx, dy = (2, 0) if axis == "x" else (0, 2)
            on_axis(dz, axis, 2, [])
            reduce_send(dz, dx, dy, "F", axis, -side)

    def r4(dz):
        side = forward_class(dz, 0)
        for d in (side, -side):
            for axis in "xy":
                dx, dy = (d, 0) if axis == "x" else (0, d)
                fulls = [arrived(dz, dx, dy, "F", axis, side)] if d == -side else []
                on_axis(dz, axis, d, fulls)
                reduce_send(dz, dx, dy, "F", axis, d)

    def z_copy(dz):
        return remote(zs.at[dz - 1], zr.at[dz - 1], z_send.at[dz - 1], z_recv.at[dz - 1],
                      near("z", dz))

    def r5(dz):
        got = [arrived(dz, 0, 0, "F", axis, came) for axis in "xy" for came in (1, -1)]
        if dz:
            total(zs.at[dz - 1], dz, 0, 0, "F", got)
            z_copy(dz).start()
        else:
            for n in (1, 2, 3):
                z_copy(n).wait_recv()
            got += [(zr.at[n], "F") for n in range(RING - 1)]
            total(out_ref, 0, 0, 0, "F", got)

    p = REDUCE_PLANES
    r1(p[0])
    r1(p[1])
    r2(p[0])
    r3(p[0])
    r1(p[2])
    r2(p[1])
    r4(p[0])
    r3(p[1])
    r1(p[3])
    r2(p[2])
    r5(p[0])
    r4(p[1])
    r3(p[2])
    r2(p[3])
    r5(p[1])
    r4(p[2])
    r3(p[3])
    r5(p[2])
    r4(p[3])
    r5(p[3])
    for copy in back_sent:
        copy.wait_send()
    for n in (1, 2, 3):
        z_copy(n).wait_send()


def delay_tables(length):
    indices = np.arange(length, dtype=np.int64)
    angle = (indices[:, None] * indices[None, :] % length) * (2.0 * np.pi / length)
    table = np.concatenate([np.cos(angle), np.sin(angle)], axis=0).astype(np.float32)
    high = table.astype(jnp.bfloat16)
    low = (table - high.astype(np.float32)).astype(jnp.bfloat16)
    return high, low


def body(sky, ker, data, block_tiles, length_bin, wedge_keep):
    per, cells = sky.shape[1], sky.shape[3]
    chans, base = data.shape[3], data.shape[2]
    shard = jnp.transpose(sky[0], (1, 0, 2)).reshape(2 * per, cells)
    high, low = delay_tables(chans)
    full = RING * RING
    vmem = pl.BlockSpec(memory_space=pltpu.VMEM)
    hbm = pl.BlockSpec(memory_space=pl.ANY)
    f32, bf16 = jnp.float32, jnp.bfloat16
    sends = 100
    out = pl.pallas_call(
        kernel,
        out_shape=jax.ShapeDtypeStruct((2 * per, cells), f32),
        in_specs=[pl.BlockSpec(memory_space=pltpu.SMEM), hbm, hbm, vmem, vmem, vmem, vmem, vmem],
        out_specs=vmem,
        scratch_shapes=[
            pltpu.VMEM((RING, full, ROWS, cells), bf16),
            pltpu.VMEM((cells, 2 * base), bf16),
            pltpu.VMEM((full * ROWS, 2 * base), f32),
            pltpu.VMEM((RING, 2, full * per, base), f32),
            pltpu.VMEM((RING, full * per, base), f32),
            pltpu.VMEM((RING, full * per, base), f32),
            pltpu.VMEM((RING, 3, full * per, base), f32),
            pltpu.VMEM((2, chans, base), f32),
            pltpu.VMEM((2 * chans, 2 * base), f32),
            pltpu.VMEM((chans, 2 * base), bf16),
            pltpu.VMEM((chans, 2 * base), bf16),
            pltpu.VMEM((chans, base), f32),
            pltpu.VMEM((2, chans, base), f32),
            pltpu.VMEM((RING, full, ROWS, 2 * base), bf16),
            pltpu.VMEM((RING, full, ROWS, cells), f32),
            pltpu.VMEM((len(HALVES), ROWS, cells // 2), bf16),
            pltpu.VMEM((len(FULLS), ROWS, cells), bf16),
            pltpu.VMEM((RING - 1, ROWS, cells), f32),
            pltpu.VMEM((RING - 1, ROWS, cells), f32),
            pltpu.SemaphoreType.DMA((3,)),
            pltpu.SemaphoreType.DMA((sends,)),
            pltpu.SemaphoreType.DMA((len(GATHER),)),
            pltpu.SemaphoreType.DMA((RING, 4)),
            pltpu.SemaphoreType.DMA((RING, 4)),
            pltpu.SemaphoreType.DMA((len(HALVES),)),
            pltpu.SemaphoreType.DMA((len(FULLS),)),
            pltpu.SemaphoreType.DMA((RING - 1,)),
            pltpu.SemaphoreType.DMA((RING - 1,)),
        ],
        compiler_params=pltpu.CompilerParams(
            collective_id=0, has_side_effects=True, vmem_limit_bytes=60 * 2**20
        ),
    )(block_tiles, shard, ker[0, 0], data[0], length_bin, wedge_keep, high, low)
    return jnp.transpose(out.reshape(2, per, cells), (1, 0, 2))[None]


def solution(mesh):
    finer = Mesh(mesh.devices.reshape(mesh.shape["tile"], RING, RING, RING), AXES)
    return jax.shard_map(
        body,
        mesh=finer,
        in_specs=(
            P("tile", FREQ, None, None),
            P("tile", FREQ, None, None, None),
            P(FREQ, None, None, None),
            P(FREQ, None),
            P(FREQ, None),
            P(),
        ),
        out_specs=P("tile", FREQ, None, None),
        check_vma=False,
    )
```

```python
import functools
import math

import jax
import jax.numpy as jnp
import numpy as np
from jax import lax
from jax.experimental import pallas as pl
from jax.experimental.pallas import tpu as pltpu
from jax.sharding import Mesh
from jax.sharding import PartitionSpec as P

FREQ = ("freq_0", "freq_1", "freq_2")
AXES = ("tile",) + FREQ
RING = 4
ROWS = 16
CORNER = 2 * RING + 2
SERVE = (
    0, 9, 12, 36, 3, 23, 48, 6, 40, 47, 22, 24, 16, 17, 41, 51, 60, 43, 84, 57, 96, 35, 46, 29,
    34, 19, 28, 94, 95, 65, 70, 54, 144, 20, 44, 64, 105, 89, 71, 83, 91, 132, 88, 31, 67, 72,
    180, 153, 32, 92, 99, 147, 108, 143, 77, 102, 156, 127, 167, 184, 68, 142, 120, 76, 136, 190,
    191, 119, 176, 112, 161, 137, 113, 150, 160, 116, 166, 175, 79, 185, 168, 124, 130, 140, 82,
    118, 80, 131, 139, 179, 128, 125, 115, 187, 188, 164, 163, 172, 178, 173,
)
ISSUE = (
    9, 48, 144, 12, 96, 3, 36, 23, 6, 47, 16, 22, 46, 40, 24, 41, 17, 35, 84, 60, 51, 57, 20, 44,
    43, 28, 34, 19, 29, 89, 65, 54, 64, 72, 70, 88, 94, 71, 95, 99, 105, 132, 108, 31, 91, 83, 67,
    92, 68, 153, 180, 156, 147, 32, 119, 143, 102, 77, 136, 120, 142, 127, 79, 175, 82, 76, 184,
    190, 191, 167, 176, 80, 128, 137, 113, 150, 185, 161, 118, 112, 140, 116, 168, 160, 166, 124,
    130, 139, 187, 179, 131, 115, 125, 188, 164, 163, 173, 172, 178,
)
RETURN = (
    116, 140, 130, 124, 125, 143, 137, 142, 118, 139, 115, 131, 92, 102, 76, 120, 136, 113, 119,
    128, 77, 188, 112, 164, 67, 88, 91, 68, 82, 65, 79, 172, 175, 127, 161, 99, 132, 108, 163, 80,
    176, 105, 178, 72, 89, 184, 71, 94, 150, 83, 167, 179, 173, 187, 64, 54, 95, 191, 160, 96, 70,
    168, 166, 32, 185, 190, 60, 57, 153, 84, 51, 180, 156, 147, 20, 31, 41, 19, 28, 29, 48, 44,
    22, 47, 144, 34, 35, 43, 6, 17, 24, 16, 23, 46, 40, 12, 3, 9, 36, 0,
)


def at(dx, dy):
    return (dx % RING) * RING + dy % RING


def decoded(code):
    return code // 48, code // 3 % 16, "FAB"[code % 3]


def side_of(dz, other):
    return 1 if (dz + other) % 2 == 0 else -1


def gather_tree():
    kids = {}

    def edge(parent, axis, step, child):
        if not (parent[0] and child[1] == CORNER):
            kids.setdefault(parent, []).append((axis, step, child))

    for step in (1, 3, 2):
        edge((0, 0, "F"), "z", step, (-step % RING, 0, "F"))
        for part in "AB":
            edge((0, CORNER, part), "z", step, (-step % RING, CORNER, part))
    for dz in range(RING):
        for turn, part in (("y", "A"), ("x", "B")):
            axis = "x" if part == "A" else "y"

            def cell(along, across):
                return at(along, across) if axis == "x" else at(across, along)

            side = side_of(dz, 0)
            for step in (1, -1):
                edge((dz, 0, "F"), axis, step, (dz, cell(-step, 0), "F"))
            edge((dz, cell(-side, 0), "F"), axis, side, (dz, cell(2, 0), "F"))
            for d in range(1, RING):
                for step in (1, -1):
                    edge((dz, cell(d, 0), "F"), turn, step, (dz, cell(d, -step), part))
                side_d = side_of(dz, d)
                edge((dz, cell(d, -side_d), part), turn, side_d, (dz, cell(d, 2), part))
    rank = {decoded(code): n for n, code in enumerate(ISSUE)}
    for children in kids.values():
        children.sort(key=lambda child: rank[child[2]])
    return kids


TREE = gather_tree()
PARENT = {child: (axis, step) for kids in TREE.values() for axis, step, child in kids}
SEMAPHORE = {message: n for n, message in enumerate(PARENT)}
HALVES = {m: n for n, m in enumerate(m for m in PARENT if m[2] != "F")}
FULLS = {m: n for n, m in enumerate(m for m in PARENT if m[2] == "F" and m[1])}


def kernel(
    bt_ref, sky_ref, ker_ref, data_ref, bins_ref, wedge_ref, thi_ref, tlo_ref, out_ref,
    buf, kc, acc, vp, t1r, hs, hr, tt, tr, vis, spec, vhi, vlo, mask, dat, u, g,
    rs_h, rs_f, zs, zr, raw, wedge, thi, tlo,
    local_sem, send_sem, ag_sem, rs_sem, t_send, t_recv,
):
    tile = lax.axis_index("tile")
    y = lax.axis_index("freq_0")
    z = lax.axis_index("freq_1")
    x = lax.axis_index("freq_2")
    cells = sky_ref.shape[1]
    half = cells // 2
    chans, base = vis.shape[1], vis.shape[2]
    per = chans // RING**3
    core = lax.rem(tile, 2)
    mate = tile + 1 - 2 * core

    def near(axis, step):
        if axis == "x":
            return (tile, y, z, lax.rem(x + step + RING, RING))
        if axis == "y":
            return (tile, lax.rem(y + step + RING, RING), z, x)
        return (tile, y, lax.rem(z + step + RING, RING), x)

    over = lax.rem(tile + 2, 4)
    peers = [near("x", 1), near("x", -1), near("y", 1), near("y", -1)]
    peers += [near("z", d) for d in (1, 2, 3)]
    peers += [(t, y, z, x) for t in (mate, over)]

    load_sky = pltpu.make_async_copy(sky_ref, buf.at[0, 0], local_sem.at[0])
    load_r = pltpu.make_async_copy(ker_ref.at[0], kc.at[:, 0:base], local_sem.at[1])
    load_i = pltpu.make_async_copy(ker_ref.at[1], kc.at[:, base : 2 * base], local_sem.at[2])
    load_sky.start()
    late = [load_r, load_i]
    for n, (src, dst) in enumerate(
        ((wedge_ref, wedge), (data_ref, raw), (thi_ref, thi), (tlo_ref, tlo))
    ):
        late.append(pltpu.make_async_copy(src, dst, local_sem.at[3 + n]))
    barrier = pltpu.get_barrier_semaphore()
    for peer in peers:
        pl.semaphore_signal(barrier, inc=1, device_id=peer, device_id_type=pl.DeviceIdType.MESH)
    for load in late:
        load.start()
    pl.semaphore_wait(barrier, len(peers))

    def part_of(ref, dz, cell, part):
        if part == "F":
            return ref.at[dz, cell]
        lo = 0 if part == "A" else half
        return ref.at[dz, cell, :, lo : lo + half]

    def remote(src, dst, send, recv, peer):
        return pltpu.make_async_remote_copy(
            src_ref=src, dst_ref=dst, send_sem=send, recv_sem=recv,
            device_id=peer, device_id_type=pl.DeviceIdType.MESH,
        )

    weight = bt_ref[0, tile].astype(jnp.float32)

    sent = []

    def gather_serve(key):
        if key in PARENT:
            ref = part_of(buf, *key)
            remote(ref, ref, send_sem.at[0], ag_sem.at[SEMAPHORE[key]], near("x", 1)).wait_recv()
        for axis, step, child in TREE.get(key, ()):
            copy = remote(
                part_of(buf, *key[:2], child[2]), part_of(buf, *child),
                send_sem.at[SEMAPHORE[child]], ag_sem.at[SEMAPHORE[child]], near(axis, step),
            )
            copy.start()
            sent.append(copy)

    depth = 512
    deep = cells // depth

    def forward(dz):
        acc[...] = jnp.zeros_like(acc)

        @pl.loop(0, deep)
        def _(k):
            lanes = pl.ds(pl.multiple_of(k * depth, depth), depth)
            rows = buf[dz, :, :, lanes].reshape(RING * RING * ROWS, depth)
            acc[...] += jnp.dot(rows, kc[lanes, :], preferred_element_type=jnp.float32)

        out = acc[...].reshape(RING * RING, 2, per, 2 * base)
        real = out[:, 0, :, :base] - out[:, 1, :, base:]
        imag = out[:, 1, :, :base] + out[:, 0, :, base:]
        vp[dz, 0] = (real * weight).reshape(RING * RING * per, base)
        vp[dz, 1] = (imag * weight).reshape(RING * RING * per, base)

    def t1(dz):
        return remote(vp.at[dz, 1 - core], t1r.at[dz], t_send.at[dz, 0], t_recv.at[dz, 0],
                      (mate, y, z, x))

    def t2(dz):
        return remote(hs.at[dz], hr.at[dz], t_send.at[dz, 1], t_recv.at[dz, 1], (over, y, z, x))

    def t3(dz):
        return remote(tt.at[dz], tr.at[dz], t_send.at[dz, 2], t_recv.at[dz, 2], (mate, y, z, x))

    def row_of(dz, cell):
        sx = lax.rem(x + cell // RING, RING)
        sy = lax.rem(y + cell % RING, RING)
        sz = lax.rem(z + dz, RING)
        return pl.multiple_of((sy * RING * RING + sz * RING + sx) * per, per)

    def tile_1(dz):
        forward(dz)
        t1(dz).start()

    def tile_2(dz):
        t1(dz).wait_recv()
        hs[dz] = vp[dz, core] + t1r[dz]
        t2(dz).start()

    def tile_3(dz):
        t2(dz).wait_recv()
        tt[dz] = hs[dz] + hr[dz]
        t3(dz).start()

    def tile_4(dz):
        t3(dz).wait_recv()
        for cell in range(RING * RING):
            mine = pl.ds(cell * per, per)
            rows = pl.ds(row_of(dz, cell), per)
            vis[core, rows, :] = tt[dz, mine, :]
            vis[1 - core, rows, :] = tr[dz, mine, :]

    def prepare():
        for load in late:
            load.wait()
        levels = lax.broadcasted_iota(jnp.int32, (wedge.shape[0], base), 0)
        hot = (levels == bins_ref[...]).astype(jnp.bfloat16)
        keep = wedge[...].astype(jnp.float32).T.astype(jnp.bfloat16)
        mask[...] = jnp.dot(keep, hot, preferred_element_type=jnp.float32)
        for plane in range(2):
            dat[plane] = raw[plane].astype(jnp.float32).T

    load_sky.wait()
    serve = [decoded(code) for code in SERVE]
    final = {key[0]: n for n, key in enumerate(serve)}
    steps = []
    for n, key in enumerate(serve):
        steps.append(functools.partial(gather_serve, key))
        if n == 4:
            steps.append(prepare)
        if final[key[0]] == n:
            steps.append(functools.partial(tile_1, key[0]))
    done = sorted(final, key=final.get)
    lag = {}
    for stage, work in ((1, tile_2), (2, tile_3), (3, tile_4)):
        for rank, dz in enumerate(done):
            lag[(rank + stage, -stage, dz)] = functools.partial(work, dz)
    tail = sorted(lag)
    shift = 0
    for rank, dz in enumerate(done):
        place = next(i for i, s in enumerate(steps) if getattr(s, "func", None) is tile_1
                     and s.args == (dz,))
        now = [lag[k] for k in tail if k[0] == rank and rank < len(done)]
        steps[place + 1 : place + 1] = now
    steps += [lag[k] for k in tail if k[0] >= len(done)]
    for step in steps:
        step()
    for copy in sent:
        copy.wait_send()
    for dz in range(RING):
        for copy in (t1(dz), t2(dz), t3(dz)):
            copy.wait_send()

    norm = 1.0 / math.sqrt(chans)
    block = 256

    def transform():
        for plane in range(2):
            lanes = slice(plane * base, (plane + 1) * base)
            whole = vis[plane]
            vhi[:, lanes] = whole.astype(jnp.bfloat16)
            vlo[:, lanes] = (whole - vhi[:, lanes].astype(jnp.float32)).astype(jnp.bfloat16)

        @pl.loop(0, 2 * chans // block)
        def _(n):
            rows = pl.ds(pl.multiple_of(n * block, block), block)
            spec[rows, :] = (
                jnp.dot(thi[rows, :], vhi[...], preferred_element_type=jnp.float32)
                + jnp.dot(thi[rows, :], vlo[...], preferred_element_type=jnp.float32)
                + jnp.dot(tlo[rows, :], vhi[...], preferred_element_type=jnp.float32)
            )

    cos_rows, sin_rows = slice(0, chans), slice(chans, 2 * chans)
    lane_r, lane_i = slice(0, base), slice(base, 2 * base)
    transform()
    vis[0] = mask[...] * (
        (spec[cos_rows, lane_r] + spec[sin_rows, lane_i]) * norm - dat[0]
    )
    vis[1] = mask[...] * (
        (spec[cos_rows, lane_i] - spec[sin_rows, lane_r]) * norm - dat[1]
    )
    transform()
    vis[0] = (spec[cos_rows, lane_r] - spec[sin_rows, lane_i]) * (norm * weight)
    vis[1] = (spec[cos_rows, lane_i] + spec[sin_rows, lane_r]) * (norm * weight)
    for dz in range(RING):
        for cell in range(RING * RING):
            rows = pl.ds(row_of(dz, cell), per)
            ur, ui = vis[0, rows, :], vis[1, rows, :]
            top = jnp.concatenate([ur, ui], axis=1)
            low = jnp.concatenate([ui, -ur], axis=1)
            u[dz, cell] = jnp.concatenate([top, low], axis=0).astype(jnp.bfloat16)

    def backward(dz, part):
        rows = u[dz].reshape(RING * RING * ROWS, 2 * base)
        first = 0 if part == "A" else deep // 2

        @pl.loop(first, first + deep // 2)
        def _(k):
            lanes = pl.ds(pl.multiple_of(k * depth, depth), depth)
            value = lax.dot_general(
                rows, kc[lanes, :], (((1,), (1,)), ((), ())),
                preferred_element_type=jnp.float32,
            )
            g[dz, :, :, lanes] = value.reshape(RING * RING, ROWS, depth)

    width = 1024

    def total(dst, dz, cell, part, terms):
        start = half if part == "B" else 0
        stop = half if part == "A" else cells

        def step_of(n):
            lanes = pl.ds(pl.multiple_of(start + n * width, width), width)
            value = g[dz, cell, :, lanes]
            for ref, kind in terms:
                shift = half if kind == "B" else 0
                own = pl.ds(pl.multiple_of(start - shift + n * width, width), width)
                value = value + ref[:, own].astype(jnp.float32)
            dst[:, lanes] = value.astype(dst.dtype)

        pl.loop(0, (stop - start) // width)(step_of)

    def returned(key):
        dz, cell, part = key
        axis, step = PARENT[key]
        step = -step % RING if axis == "z" else -step
        if cell == 0 and dz and axis == "z":
            src, dst = zs.at[dz - 1], zr.at[dz - 1]
        else:
            src = part_of(buf, *key)
            dst = rs_f.at[FULLS[key]] if part == "F" else rs_h.at[HALVES[key]]
        n = SEMAPHORE[key]
        return remote(src, dst, send_sem.at[n], rs_sem.at[n], near(axis, step)), src, dst

    ready = set()
    for code in RETURN:
        key = decoded(code)
        dz, cell, part = key
        root = key not in PARENT
        for half_part in "AB" if part == "F" else part:
            if (dz, half_part) not in ready:
                ready.add((dz, half_part))
                backward(dz, half_part)
        got = []
        for _, _, child in TREE.get(key, ()):
            copy, _, dst = returned(child)
            copy.wait_recv()
            got.append((dst, child[2]))
        whole = out_ref if root else zs.at[dz - 1] if cell == 0 else buf.at[dz, cell]
        kinds = {kind for _, kind in got}
        if part == "F" and kinds - {"F"}:
            for half_part in "AB":
                total(whole, dz, cell, half_part, [t for t in got if t[1] in ("F", half_part)])
        else:
            total(whole, dz, cell, part, got)
        if not root:
            returned(key)[0].start()
    for key in PARENT:
        returned(key)[0].wait_send()


def delay_tables(length):
    indices = np.arange(length, dtype=np.int64)
    angle = (indices[:, None] * indices[None, :] % length) * (2.0 * np.pi / length)
    table = np.concatenate([np.cos(angle), np.sin(angle)], axis=0).astype(np.float32)
    high = table.astype(jnp.bfloat16)
    low = (table - high.astype(np.float32)).astype(jnp.bfloat16)
    return high, low


def body(sky, ker, data, block_tiles, length_bin, wedge_keep):
    per, cells = sky.shape[1], sky.shape[3]
    chans, base = data.shape[3], data.shape[2]
    shard = jnp.transpose(sky[0], (1, 0, 2)).reshape(2 * per, cells)
    high, low = delay_tables(chans)
    full = RING * RING
    vmem = pl.BlockSpec(memory_space=pltpu.VMEM)
    hbm = pl.BlockSpec(memory_space=pl.ANY)
    f32, bf16 = jnp.float32, jnp.bfloat16
    out = pl.pallas_call(
        kernel,
        out_shape=jax.ShapeDtypeStruct((2 * per, cells), f32),
        in_specs=[pl.BlockSpec(memory_space=pltpu.SMEM), hbm, hbm, hbm, vmem, hbm, hbm, hbm],
        out_specs=vmem,
        scratch_shapes=[
            pltpu.VMEM((RING, full, ROWS, cells), bf16),
            pltpu.VMEM((cells, 2 * base), bf16),
            pltpu.VMEM((full * ROWS, 2 * base), f32),
            pltpu.VMEM((RING, 2, full * per, base), f32),
            pltpu.VMEM((RING, full * per, base), f32),
            pltpu.VMEM((RING, full * per, base), f32),
            pltpu.VMEM((RING, full * per, base), f32),
            pltpu.VMEM((RING, full * per, base), f32),
            pltpu.VMEM((RING, full * per, base), f32),
            pltpu.VMEM((2, chans, base), f32),
            pltpu.VMEM((2 * chans, 2 * base), f32),
            pltpu.VMEM((chans, 2 * base), bf16),
            pltpu.VMEM((chans, 2 * base), bf16),
            pltpu.VMEM((chans, base), f32),
            pltpu.VMEM((2, chans, base), f32),
            pltpu.VMEM((RING, full, ROWS, 2 * base), bf16),
            pltpu.VMEM((RING, full, ROWS, cells), f32),
            pltpu.VMEM((len(HALVES), ROWS, cells // 2), bf16),
            pltpu.VMEM((len(FULLS), ROWS, cells), bf16),
            pltpu.VMEM((RING - 1, ROWS, cells), f32),
            pltpu.VMEM((RING - 1, ROWS, cells), f32),
            pltpu.VMEM((2, base, chans), bf16),
            pltpu.VMEM(wedge_keep.shape, jnp.int32),
            pltpu.VMEM((2 * chans, chans), bf16),
            pltpu.VMEM((2 * chans, chans), bf16),
            pltpu.SemaphoreType.DMA((7,)),
            pltpu.SemaphoreType.DMA((len(PARENT),)),
            pltpu.SemaphoreType.DMA((len(PARENT),)),
            pltpu.SemaphoreType.DMA((len(PARENT),)),
            pltpu.SemaphoreType.DMA((RING, 3)),
            pltpu.SemaphoreType.DMA((RING, 3)),
        ],
        compiler_params=pltpu.CompilerParams(
            collective_id=0, has_side_effects=True, vmem_limit_bytes=60 * 2**20
        ),
    )(block_tiles, shard, ker[0, 0], data[0], length_bin, wedge_keep, high, low)
    return jnp.transpose(out.reshape(2, per, cells), (1, 0, 2))[None]


def solution(mesh):
    finer = Mesh(mesh.devices.reshape(mesh.shape["tile"], RING, RING, RING), AXES)
    return jax.shard_map(
        body,
        mesh=finer,
        in_specs=(
            P("tile", FREQ, None, None),
            P("tile", FREQ, None, None, None),
            P(FREQ, None, None, None),
            P(FREQ, None),
            P(FREQ, None),
            P(),
        ),
        out_specs=P("tile", FREQ, None, None),
        check_vma=False,
    )
```

```python
import functools
import math

import jax
import jax.numpy as jnp
import numpy as np
from jax import lax
from jax.experimental import pallas as pl
from jax.experimental.pallas import tpu as pltpu
from jax.sharding import Mesh
from jax.sharding import PartitionSpec as P

FREQ = ("freq_0", "freq_1", "freq_2")
AXES = ("tile",) + FREQ
RING = 4
ROWS = 16
GATHER_SHAPE = (
    (
        (1, -1, -1, 1, 1, -1, 1, -1),
        (-1, -1, 1, -1, -1, -1, -1, 1),
        (1, 1, -1, -1, 1, 1, -1, -1),
        (1, 1, -1, 1, -1, 1, -1, -1),
    ),
    {(0, "F"): -1, (10, "A"): 1, (10, "B"): -1, (11, "A"): 1, (14, "B"): 1},
)
REDUCE_SHAPE = (
    (
        (1, 1, -1, -1, 1, -1, 1, -1),
        (1, 1, -1, -1, 1, 1, 1, -1),
        (1, -1, -1, -1, 1, -1, -1, 1),
        (-1, 1, 1, 1, 1, -1, -1, -1),
    ),
    {(0, "F"): -1, (10, "A"): -1, (10, "B"): 1, (11, "A"): 1, (14, "B"): -1},
)
SERVE = (
    0, 3, 12, 36, 9, 17, 16, 41, 48, 22, 24, 19, 144, 23, 47, 6, 29, 46, 40, 84, 28, 34, 96, 60,
    180, 35, 51, 44, 57, 147, 43, 156, 178, 82, 20, 132, 94, 108, 153, 88, 31, 188, 168, 105, 72,
    89, 99, 65, 184, 64, 130, 70, 32, 92, 190, 54, 79, 142, 175, 160, 71, 185, 166, 118, 167, 136,
    95, 119, 80, 161, 113, 112, 191, 77, 150, 140, 143, 68, 172, 91, 120, 179, 137, 128, 102, 127,
    76, 173, 176, 187, 131, 67, 83, 163, 139, 125, 164, 115, 116, 124,
)
ISSUE = (
    144, 48, 9, 3, 12, 36, 17, 41, 16, 22, 40, 24, 46, 47, 6, 23, 29, 19, 60, 51, 96, 57, 84, 34,
    28, 180, 147, 156, 153, 35, 20, 44, 43, 88, 94, 31, 178, 82, 105, 108, 132, 99, 70, 72, 64,
    190, 184, 168, 65, 54, 89, 32, 92, 188, 95, 71, 185, 161, 160, 166, 130, 120, 136, 142, 112,
    118, 150, 191, 167, 91, 79, 175, 140, 172, 143, 119, 102, 76, 113, 137, 77, 67, 176, 80, 187,
    68, 127, 173, 163, 115, 179, 139, 83, 131, 128, 164, 124, 125, 116,
)
RETURN = (
    125, 140, 116, 115, 119, 131, 118, 127, 124, 187, 137, 139, 113, 173, 102, 143, 128, 163, 112,
    172, 80, 188, 120, 142, 185, 68, 164, 136, 179, 99, 79, 105, 176, 83, 108, 77, 76, 190, 166,
    67, 184, 82, 132, 91, 150, 94, 161, 130, 168, 167, 160, 54, 191, 175, 89, 92, 72, 96, 64, 88,
    65, 32, 95, 147, 71, 70, 156, 180, 153, 51, 60, 31, 84, 57, 43, 46, 178, 47, 19, 20, 144, 29,
    44, 48, 34, 28, 35, 6, 41, 22, 16, 17, 24, 40, 23, 9, 12, 3, 36, 0,
)
GROUPS = (16, 16, 16, 8, 8)


def at(dx, dy):
    return (dx % RING) * RING + dy % RING


def decoded(code):
    return code // 48, code // 3 % 16, "FAB"[code % 3]


def message_tree(shape):
    sides, by_z = shape
    kids = {}

    def edge(parent, axis, step, child):
        if axis == "z" or not (child[0] and child[1:] in by_z):
            kids.setdefault(parent, []).append((axis, step, child))

    for what, side in by_z.items():
        edge((0, *what), "z", -1, (1, *what))
        edge((0, *what), "z", 1, (3, *what))
        edge((2 + side, *what), "z", side, (2, *what))
    for dz in range(RING):
        for turn, part in (("y", "A"), ("x", "B")):
            axis, first = ("x", 0) if part == "A" else ("y", RING)

            def cell(along, across):
                return at(along, across) if axis == "x" else at(across, along)

            side = sides[dz][0]
            for step in (1, -1):
                edge((dz, 0, "F"), axis, step, (dz, cell(-step, 0), "F"))
            edge((dz, cell(-side, 0), "F"), axis, side, (dz, cell(2, 0), "F"))
            for d in range(1, RING):
                for step in (1, -1):
                    edge((dz, cell(d, 0), "F"), turn, step, (dz, cell(d, -step), part))
                side_d = sides[dz][first + d]
                edge((dz, cell(d, -side_d), part), turn, side_d, (dz, cell(d, 2), part))
    return kids


def parents(kids):
    return {child: (axis, step) for edges in kids.values() for axis, step, child in edges}


DOWN = message_tree(GATHER_SHAPE)
for edges in DOWN.values():
    edges.sort(key=lambda edge: ISSUE.index((edge[2][0] * 16 + edge[2][1]) * 3 + "FAB".index(edge[2][2])))
UP = message_tree(REDUCE_SHAPE)
SERVED_BY = parents(DOWN)
RETURNED_BY = parents(UP)
SEMAPHORE = {message: n for n, message in enumerate(SERVED_BY)}
HALVES = {m: n for n, m in enumerate(m for m in SERVED_BY if m[2] != "F")}
FULLS = {m: n for n, m in enumerate(m for m in SERVED_BY if m[2] == "F" and m[1])}


def kernel(
    bt_ref, sky_ref, ker_ref, data_ref, bins_ref, wedge_ref, thi_ref, tlo_ref, out_ref,
    buf, kc, acc, vp, t1r, hs, hr, vis, spec, vhi, vlo, mask, dat, u, g,
    rs_h, rs_f, zs, zr, raw_sky, raw, wedge, thi, tlo,
    local_sem, send_sem, ag_sem, rs_sem, t_send, t_recv,
):
    tile = lax.axis_index("tile")
    y = lax.axis_index("freq_0")
    z = lax.axis_index("freq_1")
    x = lax.axis_index("freq_2")
    cells = sky_ref.shape[2]
    half = cells // 2
    chans, base = vis.shape[1], vis.shape[2]
    per = chans // RING**3
    core = lax.rem(tile, 2)
    mate = tile + 1 - 2 * core

    def near(axis, step):
        if axis == "x":
            return (tile, y, z, lax.rem(x + step + RING, RING))
        if axis == "y":
            return (tile, lax.rem(y + step + RING, RING), z, x)
        return (tile, y, lax.rem(z + step + RING, RING), x)

    over = lax.rem(tile + 2, 4)
    cross = lax.rem(mate + 2, 4)
    peers = [near("x", 1), near("x", -1), near("y", 1), near("y", -1)]
    peers += [near("z", 1), near("z", -1)]
    peers += [(t, y, z, x) for t in (mate, over, cross)]

    load_sky = pltpu.make_async_copy(sky_ref, raw_sky, local_sem.at[0])
    load_r = pltpu.make_async_copy(ker_ref.at[0], kc.at[:, 0:base], local_sem.at[1])
    load_i = pltpu.make_async_copy(ker_ref.at[1], kc.at[:, base : 2 * base], local_sem.at[2])
    load_sky.start()
    late = [load_r, load_i]
    for n, (src, dst) in enumerate(
        ((wedge_ref, wedge), (data_ref, raw), (thi_ref, thi), (tlo_ref, tlo))
    ):
        late.append(pltpu.make_async_copy(src, dst, local_sem.at[3 + n]))
    barrier = pltpu.get_barrier_semaphore()
    for peer in peers:
        pl.semaphore_signal(barrier, inc=1, device_id=peer, device_id_type=pl.DeviceIdType.MESH)
    for load in late:
        load.start()
    load_sky.wait()
    buf[0, 0] = jnp.concatenate(
        [raw_sky[:, plane, :].astype(jnp.float32) for plane in range(2)], axis=0
    ).astype(jnp.bfloat16)
    pl.semaphore_wait(barrier, len(peers))

    def part_of(ref, dz, cell, part):
        if part == "F":
            return ref.at[dz, cell]
        lo = 0 if part == "A" else half
        return ref.at[dz, cell, :, lo : lo + half]

    def remote(src, dst, send, recv, peer):
        return pltpu.make_async_remote_copy(
            src_ref=src, dst_ref=dst, send_sem=send, recv_sem=recv,
            device_id=peer, device_id_type=pl.DeviceIdType.MESH,
        )

    weight = bt_ref[0, tile].astype(jnp.float32)

    sent = []

    def gather_serve(key):
        if key in SERVED_BY:
            ref = part_of(buf, *key)
            remote(ref, ref, send_sem.at[0], ag_sem.at[SEMAPHORE[key]], near("x", 1)).wait_recv()
        for axis, step, child in DOWN.get(key, ()):
            copy = remote(
                part_of(buf, *key[:2], child[2]), part_of(buf, *child),
                send_sem.at[SEMAPHORE[child]], ag_sem.at[SEMAPHORE[child]], near(axis, step),
            )
            copy.start()
            sent.append(copy)

    depth = 512
    deep = cells // depth

    def forward(shards, place):
        count = len(shards)
        rows = pl.ds(0, count * ROWS)
        acc[rows, :] = jnp.zeros((count * ROWS, 2 * base), jnp.float32)

        @pl.loop(0, deep)
        def _(k):
            lanes = pl.ds(pl.multiple_of(k * depth, depth), depth)
            value = jnp.concatenate([buf[dz, cell, :, lanes] for dz, cell in shards], axis=0)
            acc[rows, :] += jnp.dot(value, kc[lanes, :], preferred_element_type=jnp.float32)

        out = acc[rows, :].reshape(count, 2, per, 2 * base)
        real = out[:, 0, :, :base] - out[:, 1, :, base:]
        imag = out[:, 1, :, :base] + out[:, 0, :, base:]
        vp[0, place, :] = (real * weight).reshape(count * per, base)
        vp[1, place, :] = (imag * weight).reshape(count * per, base)

    def t1(n, place):
        return remote(vp.at[1 - core, place], t1r.at[place], t_send.at[n, 0], t_recv.at[n, 0],
                      (mate, y, z, x))

    def t2(n, place):
        return [
            remote(hs.at[place], hr.at[k, place], t_send.at[n, k + 1], t_recv.at[n, k + 1],
                   (t, y, z, x))
            for k, t in enumerate((over, cross, mate))
        ]

    def row_of(dz, cell):
        sx = lax.rem(x + cell // RING, RING)
        sy = lax.rem(y + cell % RING, RING)
        sz = lax.rem(z + dz, RING)
        return pl.multiple_of((sy * RING * RING + sz * RING + sx) * per, per)

    def tile_1(n, shards, place):
        forward(shards, place)
        t1(n, place).start()

    def tile_2(n, shards, place):
        t1(n, place).wait_recv()
        hs[place, :] = vp[core, place, :] + t1r[place, :]
        for copy in t2(n, place):
            copy.start()

    def tile_3(n, shards, place):
        for copy in t2(n, place):
            copy.wait_recv()
        for k, shard in enumerate(shards):
            mine = slice(place.start + k * per, place.start + (k + 1) * per)
            rows = pl.ds(row_of(*shard), per)
            vis[core, rows, :] = hs[mine, :] + hr[0, mine, :]
            vis[1 - core, rows, :] = hr[2, mine, :] + hr[1, mine, :]

    def prepare():
        for load in late:
            load.wait()
        levels = lax.broadcasted_iota(jnp.int32, (wedge.shape[0], base), 0)
        hot = (levels == bins_ref[...]).astype(jnp.bfloat16)
        keep = wedge[...].astype(jnp.float32).T.astype(jnp.bfloat16)
        mask[...] = jnp.dot(keep, hot, preferred_element_type=jnp.float32)
        for plane in range(2):
            dat[plane] = raw[plane].astype(jnp.float32).T

    serve = [decoded(code) for code in SERVE]
    whole = {}
    for n, key in enumerate(serve):
        whole[key[:2]] = n
    order = sorted(whole, key=whole.get)
    plan = {n: [functools.partial(gather_serve, key)] for n, key in enumerate(serve)}
    plan[4].append(prepare)
    groups = []
    start = 0
    for n, count in enumerate(GROUPS):
        shards = order[start : start + count]
        groups.append((n, shards, slice(start * per, (start + count) * per)))
        start += count
        last = max(whole[shard] for shard in shards)
        final = n == len(GROUPS) - 1
        for work, lag in ((tile_1, 0), (tile_2, 8), (tile_3, 24)):
            spot = last + lag if not final else len(serve) + lag
            plan.setdefault(spot, []).append(functools.partial(work, *groups[-1]))
    for spot in sorted(plan):
        for step in plan[spot]:
            step()
    for copy in sent:
        copy.wait_send()
    for n, _, place in groups:
        for copy in (t1(n, place), *t2(n, place)):
            copy.wait_send()

    norm = 1.0 / math.sqrt(chans)
    block = 256

    def transform():
        for plane in range(2):
            lanes = slice(plane * base, (plane + 1) * base)
            whole = vis[plane]
            vhi[:, lanes] = whole.astype(jnp.bfloat16)
            vlo[:, lanes] = (whole - vhi[:, lanes].astype(jnp.float32)).astype(jnp.bfloat16)

        @pl.loop(0, 2 * chans // block)
        def _(n):
            rows = pl.ds(pl.multiple_of(n * block, block), block)
            spec[rows, :] = (
                jnp.dot(thi[rows, :], vhi[...], preferred_element_type=jnp.float32)
                + jnp.dot(thi[rows, :], vlo[...], preferred_element_type=jnp.float32)
                + jnp.dot(tlo[rows, :], vhi[...], preferred_element_type=jnp.float32)
            )

    cos_rows, sin_rows = slice(0, chans), slice(chans, 2 * chans)
    lane_r, lane_i = slice(0, base), slice(base, 2 * base)
    transform()
    vis[0] = mask[...] * (
        (spec[cos_rows, lane_r] + spec[sin_rows, lane_i]) * norm - dat[0]
    )
    vis[1] = mask[...] * (
        (spec[cos_rows, lane_i] - spec[sin_rows, lane_r]) * norm - dat[1]
    )
    transform()
    vis[0] = (spec[cos_rows, lane_r] - spec[sin_rows, lane_i]) * (norm * weight)
    vis[1] = (spec[cos_rows, lane_i] + spec[sin_rows, lane_r]) * (norm * weight)
    for dz in range(RING):
        for cell in range(RING * RING):
            rows = pl.ds(row_of(dz, cell), per)
            ur, ui = vis[0, rows, :], vis[1, rows, :]
            top = jnp.concatenate([ur, ui], axis=1)
            low = jnp.concatenate([ui, -ur], axis=1)
            u[dz, cell] = jnp.concatenate([top, low], axis=0).astype(jnp.bfloat16)

    def backward(dz, part):
        rows = u[dz].reshape(RING * RING * ROWS, 2 * base)
        first = 0 if part == "A" else deep // 2

        @pl.loop(first, first + deep // 2)
        def _(k):
            lanes = pl.ds(pl.multiple_of(k * depth, depth), depth)
            value = lax.dot_general(
                rows, kc[lanes, :], (((1,), (1,)), ((), ())),
                preferred_element_type=jnp.float32,
            )
            g[dz, :, :, lanes] = value.reshape(RING * RING, ROWS, depth)

    width = 1024

    def total(dst, dz, cell, part, terms):
        start = half if part == "B" else 0
        stop = half if part == "A" else cells

        def step_of(n):
            lanes = pl.ds(pl.multiple_of(start + n * width, width), width)
            value = g[dz, cell, :, lanes]
            for ref, kind in terms:
                shift = half if kind == "B" else 0
                own = pl.ds(pl.multiple_of(start - shift + n * width, width), width)
                value = value + ref[:, own].astype(jnp.float32)
            dst[:, lanes] = value.astype(dst.dtype)

        pl.loop(0, (stop - start) // width)(step_of)

    def returned(key):
        dz, cell, part = key
        axis, step = RETURNED_BY[key]
        if cell == 0 and dz and axis == "z":
            src, dst = zs.at[dz - 1], zr.at[dz - 1]
        else:
            src = part_of(buf, *key)
            dst = rs_f.at[FULLS[key]] if part == "F" else rs_h.at[HALVES[key]]
        n = SEMAPHORE[key]
        return remote(src, dst, send_sem.at[n], rs_sem.at[n], near(axis, -step)), src, dst

    ready = set()
    for code in RETURN:
        key = decoded(code)
        dz, cell, part = key
        root = key not in RETURNED_BY
        for half_part in "AB" if part == "F" else part:
            if (dz, half_part) not in ready:
                ready.add((dz, half_part))
                backward(dz, half_part)
        got = []
        for _, _, child in UP.get(key, ()):
            copy, _, dst = returned(child)
            copy.wait_recv()
            got.append((dst, child[2]))
        whole = out_ref if root else zs.at[dz - 1] if cell == 0 else buf.at[dz, cell]
        kinds = {kind for _, kind in got}
        if part == "F" and kinds - {"F"}:
            for half_part in "AB":
                total(whole, dz, cell, half_part, [t for t in got if t[1] in ("F", half_part)])
        else:
            total(whole, dz, cell, part, got)
        if not root:
            returned(key)[0].start()
    for key in RETURNED_BY:
        returned(key)[0].wait_send()


def delay_tables(length):
    indices = np.arange(length, dtype=np.int64)
    angle = (indices[:, None] * indices[None, :] % length) * (2.0 * np.pi / length)
    table = np.concatenate([np.cos(angle), np.sin(angle)], axis=0).astype(np.float32)
    high = table.astype(jnp.bfloat16)
    low = (table - high.astype(np.float32)).astype(jnp.bfloat16)
    return high, low


def body(sky, ker, data, block_tiles, length_bin, wedge_keep):
    per, cells = sky.shape[1], sky.shape[3]
    chans, base = data.shape[3], data.shape[2]
    high, low = delay_tables(chans)
    full = RING * RING
    vmem = pl.BlockSpec(memory_space=pltpu.VMEM)
    hbm = pl.BlockSpec(memory_space=pl.ANY)
    f32, bf16 = jnp.float32, jnp.bfloat16
    out = pl.pallas_call(
        kernel,
        out_shape=jax.ShapeDtypeStruct((2 * per, cells), f32),
        in_specs=[pl.BlockSpec(memory_space=pltpu.SMEM), hbm, hbm, hbm, vmem, hbm, hbm, hbm],
        out_specs=vmem,
        scratch_shapes=[
            pltpu.VMEM((RING, full, ROWS, cells), bf16),
            pltpu.VMEM((cells, 2 * base), bf16),
            pltpu.VMEM((full * ROWS, 2 * base), f32),
            pltpu.VMEM((2, chans, base), f32),
            pltpu.VMEM((chans, base), f32),
            pltpu.VMEM((chans, base), f32),
            pltpu.VMEM((3, chans, base), f32),
            pltpu.VMEM((2, chans, base), f32),
            pltpu.VMEM((2 * chans, 2 * base), f32),
            pltpu.VMEM((chans, 2 * base), bf16),
            pltpu.VMEM((chans, 2 * base), bf16),
            pltpu.VMEM((chans, base), f32),
            pltpu.VMEM((2, chans, base), f32),
            pltpu.VMEM((RING, full, ROWS, 2 * base), bf16),
            pltpu.VMEM((RING, full, ROWS, cells), f32),
            pltpu.VMEM((len(HALVES), ROWS, cells // 2), bf16),
            pltpu.VMEM((len(FULLS), ROWS, cells), bf16),
            pltpu.VMEM((RING - 1, ROWS, cells), f32),
            pltpu.VMEM((RING - 1, ROWS, cells), f32),
            pltpu.VMEM((per, 2, cells), bf16),
            pltpu.VMEM((2, base, chans), bf16),
            pltpu.VMEM(wedge_keep.shape, jnp.int32),
            pltpu.VMEM((2 * chans, chans), bf16),
            pltpu.VMEM((2 * chans, chans), bf16),
            pltpu.SemaphoreType.DMA((7,)),
            pltpu.SemaphoreType.DMA((len(SEMAPHORE),)),
            pltpu.SemaphoreType.DMA((len(SEMAPHORE),)),
            pltpu.SemaphoreType.DMA((len(SEMAPHORE),)),
            pltpu.SemaphoreType.DMA((len(GROUPS), 4)),
            pltpu.SemaphoreType.DMA((len(GROUPS), 4)),
        ],
        compiler_params=pltpu.CompilerParams(
            collective_id=0, has_side_effects=True, vmem_limit_bytes=60 * 2**20
        ),
    )(block_tiles, sky[0], ker[0, 0], data[0], length_bin, wedge_keep, high, low)
    return jnp.transpose(out.reshape(2, per, cells), (1, 0, 2))[None]


def solution(mesh):
    finer = Mesh(mesh.devices.reshape(mesh.shape["tile"], RING, RING, RING), AXES)
    return jax.shard_map(
        body,
        mesh=finer,
        in_specs=(
            P("tile", FREQ, None, None),
            P("tile", FREQ, None, None, None),
            P(FREQ, None, None, None),
            P(FREQ, None),
            P(FREQ, None),
            P(),
        ),
        out_specs=P("tile", FREQ, None, None),
        check_vma=False,
    )
```

```python
import functools
import math

import jax
import jax.numpy as jnp
import numpy as np
from jax import lax
from jax.experimental import pallas as pl
from jax.experimental.pallas import tpu as pltpu
from jax.sharding import Mesh
from jax.sharding import PartitionSpec as P

FREQ = ("freq_0", "freq_1", "freq_2")
AXES = ("tile",) + FREQ
RING = 4
ROWS = 16
GATHER_SHAPE = (
    (
        (1, 1, -1, -1, -1, 1, 1, -1),
        (-1, 1, 1, 1, -1, -1, -1, -1),
        (1, 1, 1, -1, 1, -1, -1, 1),
        (1, -1, -1, -1, -1, -1, 1, 1),
    ),
    {(0, "F"): -1, (10, "A"): 1, (10, "B"): -1, (11, "A"): 1, (14, "B"): 1},
)
REDUCE_SHAPE = (
    (
        (1, -1, -1, 1, 1, -1, 1, -1),
        (1, -1, -1, 1, -1, 1, -1, -1),
        (1, 1, 1, 1, 1, 1, -1, 1),
        (-1, -1, -1, -1, -1, -1, -1, -1),
    ),
    {(0, "F"): -1, (10, "A"): 1, (10, "B"): 1, (11, "A"): -1, (14, "B"): 1},
)
SERVE = (
    0, 9, 36, 3, 12, 23, 40, 48, 6, 24, 35, 43, 144, 22, 47, 16, 17, 41, 46, 57, 51, 20, 28, 44,
    -16, 96, 34, 156, 60, -32, 153, 84, 71, 29, 19, 54, 147, 180, 31, 89, 108, 188, -48, 82, 65,
    166, 32, 99, 105, -64, 95, 92, 160, 178, 70, -17, 167, 132, 175, 150, 191, 79, 72, -33, 64,
    94, 185, 68, 140, 83, 190, 161, 88, 112, 118, 168, 163, 80, 184, 176, 137, 77, 113, 136, -18,
    143, 119, 102, 130, -34, 164, 172, 67, 120, 173, 128, 142, 76, 187, -49, 127, 91, 179, -19,
    125, 139, -65, -50, 115, 131, 116, 124, -20, -35, -66, -36, -51, -52, -67, -68,
)
ISSUE = (
    48, 9, 36, 3, 12, 144, 6, 23, 47, 40, 46, 24, 17, 41, 22, 16, 35, 43, 60, 96, 51, 84, 57, 20,
    44, 34, 28, 147, 180, 153, 156, 19, 29, 71, 95, 65, 89, 54, 31, 92, 188, 32, 105, 99, 108,
    132, 178, 82, 160, 166, 70, 72, 64, 191, 150, 167, 94, 88, 83, 68, 185, 161, 184, 168, 190,
    79, 175, 112, 118, 140, 77, 80, 176, 137, 113, 119, 102, 143, 163, 130, 67, 142, 120, 136,
    127, 164, 179, 76, 91, 173, 115, 172, 128, 187, 125, 139, 131, 116, 124,
)
RETURN = (
    125, 124, 116, 112, 115, 113, 68, 139, 131, 179, 130, 83, 127, 137, 136, 120, 118, 119, 128,
    76, 80, 142, 187, 102, 79, 143, 172, 77, 91, 173, 82, 99, 132, 108, 105, 67, 140, 191, 89,
    167, 163, 164, 65, 176, 190, 72, 71, 92, 54, 88, 70, 184, 64, 95, 161, 160, 96, 168, 178, 94,
    32, 185, 175, 166, 150, 51, 57, 60, 84, 188, 153, 156, 180, 47, 147, 43, 44, 31, 34, 22, 19,
    29, 20, 48, 144, 41, 28, 35, 16, 6, 46, 17, 24, 40, 23, 12, 3, 9, 36, 0,
)
GROUPS = (16, 16, 16, 12, 4)


def at(dx, dy):
    return (dx % RING) * RING + dy % RING


def decoded(code):
    return code // 48, code // 3 % 16, "FAB"[code % 3]


def message_tree(shape):
    sides, by_z = shape
    kids = {}

    def edge(parent, axis, step, child):
        if axis == "z" or not (child[0] and child[1:] in by_z):
            kids.setdefault(parent, []).append((axis, step, child))

    for what, side in by_z.items():
        edge((0, *what), "z", -1, (1, *what))
        edge((0, *what), "z", 1, (3, *what))
        edge((2 + side, *what), "z", side, (2, *what))
    for dz in range(RING):
        for turn, part in (("y", "A"), ("x", "B")):
            axis, first = ("x", 0) if part == "A" else ("y", RING)

            def cell(along, across):
                return at(along, across) if axis == "x" else at(across, along)

            side = sides[dz][0]
            for step in (1, -1):
                edge((dz, 0, "F"), axis, step, (dz, cell(-step, 0), "F"))
            edge((dz, cell(-side, 0), "F"), axis, side, (dz, cell(2, 0), "F"))
            for d in range(1, RING):
                for step in (1, -1):
                    edge((dz, cell(d, 0), "F"), turn, step, (dz, cell(d, -step), part))
                side_d = sides[dz][first + d]
                edge((dz, cell(d, -side_d), part), turn, side_d, (dz, cell(d, 2), part))
    return kids


def coded(message):
    return (message[0] * 16 + message[1]) * 3 + "FAB".index(message[2])


def parents(kids):
    return {child: (axis, step) for edges in kids.values() for axis, step, child in edges}


DOWN = message_tree(GATHER_SHAPE)
for edges in DOWN.values():
    edges.sort(key=lambda edge: ISSUE.index(coded(edge[2])))
UP = message_tree(REDUCE_SHAPE)
SERVED_BY = parents(DOWN)
RETURNED_BY = parents(UP)
SEMAPHORE = {message: n for n, message in enumerate(SERVED_BY)}
HALVES = {m: n for n, m in enumerate(m for m in SERVED_BY if m[2] != "F")}
FULLS = {m: n for n, m in enumerate(m for m in SERVED_BY if m[2] == "F" and m[1])}


def kernel(
    bt_ref, sky_ref, ker_ref, data_ref, bins_ref, wedge_ref, thi_ref, tlo_ref, out_ref,
    buf, kc, acc, vp, t1r, hs, hr, tt, tr, vis, spec, vhi, vlo, mask, dat, u, g,
    rs_h, rs_f, zs, zr, raw_sky, raw, wedge, thi, tlo,
    local_sem, send_sem, ag_sem, rs_sem, t_send, t_recv,
):
    tile = lax.axis_index("tile")
    y = lax.axis_index("freq_0")
    z = lax.axis_index("freq_1")
    x = lax.axis_index("freq_2")
    cells = sky_ref.shape[2]
    half = cells // 2
    chans, base = vis.shape[1], vis.shape[2]
    per = chans // RING**3
    core = lax.rem(tile, 2)
    mate = tile + 1 - 2 * core

    def near(axis, step):
        if axis == "x":
            return (tile, y, z, lax.rem(x + step + RING, RING))
        if axis == "y":
            return (tile, lax.rem(y + step + RING, RING), z, x)
        return (tile, y, lax.rem(z + step + RING, RING), x)

    over = lax.rem(tile + 2, 4)
    peers = [near("x", 1), near("x", -1), near("y", 1), near("y", -1)]
    peers += [near("z", 1), near("z", -1)]
    peers += [(t, y, z, x) for t in (mate, over)]

    load_sky = pltpu.make_async_copy(sky_ref, raw_sky, local_sem.at[0])
    load_r = pltpu.make_async_copy(ker_ref.at[0], kc.at[:, 0:base], local_sem.at[1])
    load_i = pltpu.make_async_copy(ker_ref.at[1], kc.at[:, base : 2 * base], local_sem.at[2])
    load_sky.start()
    late = [load_r, load_i]
    for n, (src, dst) in enumerate(
        ((wedge_ref, wedge), (data_ref, raw), (thi_ref, thi), (tlo_ref, tlo))
    ):
        late.append(pltpu.make_async_copy(src, dst, local_sem.at[3 + n]))
    barrier = pltpu.get_barrier_semaphore()
    for peer in peers:
        pl.semaphore_signal(barrier, inc=1, device_id=peer, device_id_type=pl.DeviceIdType.MESH)
    for load in late:
        load.start()
    load_sky.wait()
    buf[0, 0] = jnp.concatenate(
        [raw_sky[:, plane, :].astype(jnp.float32) for plane in range(2)], axis=0
    ).astype(jnp.bfloat16)
    pl.semaphore_wait(barrier, len(peers))

    def part_of(ref, dz, cell, part):
        if part == "F":
            return ref.at[dz, cell]
        lo = 0 if part == "A" else half
        return ref.at[dz, cell, :, lo : lo + half]

    def remote(src, dst, send, recv, peer):
        return pltpu.make_async_remote_copy(
            src_ref=src, dst_ref=dst, send_sem=send, recv_sem=recv,
            device_id=peer, device_id_type=pl.DeviceIdType.MESH,
        )

    weight = bt_ref[0, tile].astype(jnp.float32)

    sent = []

    def gather_serve(key):
        if key in SERVED_BY:
            ref = part_of(buf, *key)
            remote(ref, ref, send_sem.at[0], ag_sem.at[SEMAPHORE[key]], near("x", 1)).wait_recv()
        for axis, step, child in DOWN.get(key, ()):
            copy = remote(
                part_of(buf, *key[:2], child[2]), part_of(buf, *child),
                send_sem.at[SEMAPHORE[child]], ag_sem.at[SEMAPHORE[child]], near(axis, step),
            )
            copy.start()
            sent.append(copy)

    depth = 512
    deep = cells // depth

    def forward(shards, place):
        count = len(shards)
        rows = pl.ds(0, count * ROWS)
        acc[rows, :] = jnp.zeros((count * ROWS, 2 * base), jnp.float32)

        @pl.loop(0, deep)
        def _(k):
            lanes = pl.ds(pl.multiple_of(k * depth, depth), depth)
            value = jnp.concatenate([buf[dz, cell, :, lanes] for dz, cell in shards], axis=0)
            acc[rows, :] += jnp.dot(value, kc[lanes, :], preferred_element_type=jnp.float32)

        out = acc[rows, :].reshape(count, 2, per, 2 * base)
        real = out[:, 0, :, :base] - out[:, 1, :, base:]
        imag = out[:, 1, :, :base] + out[:, 0, :, base:]
        vp[0, place, :] = (real * weight).reshape(count * per, base)
        vp[1, place, :] = (imag * weight).reshape(count * per, base)

    def t1(n, place):
        return remote(vp.at[1 - core, place], t1r.at[place], t_send.at[n, 0], t_recv.at[n, 0],
                      (mate, y, z, x))

    def t2(n, place):
        return remote(hs.at[place], hr.at[place], t_send.at[n, 1], t_recv.at[n, 1],
                      (over, y, z, x))

    def t3(n, place):
        return remote(tt.at[place], tr.at[place], t_send.at[n, 2], t_recv.at[n, 2],
                      (mate, y, z, x))

    def row_of(dz, cell):
        sx = lax.rem(x + cell // RING, RING)
        sy = lax.rem(y + cell % RING, RING)
        sz = lax.rem(z + dz, RING)
        return pl.multiple_of((sy * RING * RING + sz * RING + sx) * per, per)

    def tile_1(n, shards, place):
        forward(shards, place)
        t1(n, place).start()

    def tile_2(n, shards, place):
        t1(n, place).wait_recv()
        hs[place, :] = vp[core, place, :] + t1r[place, :]
        t2(n, place).start()

    def tile_3(n, shards, place):
        t2(n, place).wait_recv()
        tt[place, :] = hs[place, :] + hr[place, :]
        t3(n, place).start()

    def tile_4(n, shards, place):
        t3(n, place).wait_recv()
        for k, shard in enumerate(shards):
            mine = slice(place.start + k * per, place.start + (k + 1) * per)
            rows = pl.ds(row_of(*shard), per)
            vis[core, rows, :] = tt[mine, :]
            vis[1 - core, rows, :] = tr[mine, :]

    def prepare():
        for load in late:
            load.wait()
        levels = lax.broadcasted_iota(jnp.int32, (wedge.shape[0], base), 0)
        hot = (levels == bins_ref[...]).astype(jnp.bfloat16)
        keep = wedge[...].astype(jnp.float32).T.astype(jnp.bfloat16)
        mask[...] = jnp.dot(keep, hot, preferred_element_type=jnp.float32)
        for plane in range(2):
            dat[plane] = raw[plane].astype(jnp.float32).T

    whole = {}
    for n, code in enumerate(SERVE):
        if code >= 0:
            whole[decoded(code)[:2]] = n
    order = sorted(whole, key=whole.get)
    groups = []
    start = 0
    for n, count in enumerate(GROUPS):
        place = slice(start * per, (start + count) * per)
        groups.append((n, order[start : start + count], place))
        start += count
    for n, code in enumerate(SERVE):
        if code >= 0:
            gather_serve(decoded(code))
        else:
            (tile_1, tile_2, tile_3, tile_4)[-code // 16 - 1](*groups[-code % 16])
        if n == 4:
            prepare()
    for copy in sent:
        copy.wait_send()
    for n, _, place in groups:
        for copy in (t1(n, place), t2(n, place), t3(n, place)):
            copy.wait_send()

    norm = 1.0 / math.sqrt(chans)
    block = 256

    def transform():
        for plane in range(2):
            lanes = slice(plane * base, (plane + 1) * base)
            whole = vis[plane]
            vhi[:, lanes] = whole.astype(jnp.bfloat16)
            vlo[:, lanes] = (whole - vhi[:, lanes].astype(jnp.float32)).astype(jnp.bfloat16)

        @pl.loop(0, 2 * chans // block)
        def _(n):
            rows = pl.ds(pl.multiple_of(n * block, block), block)
            spec[rows, :] = (
                jnp.dot(thi[rows, :], vhi[...], preferred_element_type=jnp.float32)
                + jnp.dot(thi[rows, :], vlo[...], preferred_element_type=jnp.float32)
                + jnp.dot(tlo[rows, :], vhi[...], preferred_element_type=jnp.float32)
            )

    cos_rows, sin_rows = slice(0, chans), slice(chans, 2 * chans)
    lane_r, lane_i = slice(0, base), slice(base, 2 * base)
    transform()
    vis[0] = mask[...] * (
        (spec[cos_rows, lane_r] + spec[sin_rows, lane_i]) * norm - dat[0]
    )
    vis[1] = mask[...] * (
        (spec[cos_rows, lane_i] - spec[sin_rows, lane_r]) * norm - dat[1]
    )
    transform()
    vis[0] = (spec[cos_rows, lane_r] - spec[sin_rows, lane_i]) * (norm * weight)
    vis[1] = (spec[cos_rows, lane_i] + spec[sin_rows, lane_r]) * (norm * weight)
    for dz in range(RING):
        for cell in range(RING * RING):
            rows = pl.ds(row_of(dz, cell), per)
            ur, ui = vis[0, rows, :], vis[1, rows, :]
            top = jnp.concatenate([ur, ui], axis=1)
            low = jnp.concatenate([ui, -ur], axis=1)
            u[dz, cell] = jnp.concatenate([top, low], axis=0).astype(jnp.bfloat16)

    def backward(dz, part):
        rows = u[dz].reshape(RING * RING * ROWS, 2 * base)
        first = 0 if part == "A" else deep // 2

        @pl.loop(first, first + deep // 2)
        def _(k):
            lanes = pl.ds(pl.multiple_of(k * depth, depth), depth)
            value = lax.dot_general(
                rows, kc[lanes, :], (((1,), (1,)), ((), ())),
                preferred_element_type=jnp.float32,
            )
            g[dz, :, :, lanes] = value.reshape(RING * RING, ROWS, depth)

    width = 1024

    def total(dst, dz, cell, part, terms):
        start = half if part == "B" else 0
        stop = half if part == "A" else cells

        def step_of(n):
            lanes = pl.ds(pl.multiple_of(start + n * width, width), width)
            value = g[dz, cell, :, lanes]
            for ref, kind in terms:
                shift = half if kind == "B" else 0
                own = pl.ds(pl.multiple_of(start - shift + n * width, width), width)
                value = value + ref[:, own].astype(jnp.float32)
            dst[:, lanes] = value.astype(dst.dtype)

        pl.loop(0, (stop - start) // width)(step_of)

    def returned(key):
        dz, cell, part = key
        axis, step = RETURNED_BY[key]
        if cell == 0 and dz and axis == "z":
            src, dst = zs.at[dz - 1], zr.at[dz - 1]
        else:
            src = part_of(buf, *key)
            dst = rs_f.at[FULLS[key]] if part == "F" else rs_h.at[HALVES[key]]
        n = SEMAPHORE[key]
        return remote(src, dst, send_sem.at[n], rs_sem.at[n], near(axis, -step)), src, dst

    ready = set()
    for code in RETURN:
        key = decoded(code)
        dz, cell, part = key
        root = key not in RETURNED_BY
        for half_part in "AB" if part == "F" else part:
            if (dz, half_part) not in ready:
                ready.add((dz, half_part))
                backward(dz, half_part)
        got = []
        for _, _, child in UP.get(key, ()):
            copy, _, dst = returned(child)
            copy.wait_recv()
            got.append((dst, child[2]))
        whole = out_ref if root else zs.at[dz - 1] if cell == 0 else buf.at[dz, cell]
        kinds = {kind for _, kind in got}
        if part == "F" and kinds - {"F"}:
            for half_part in "AB":
                total(whole, dz, cell, half_part, [t for t in got if t[1] in ("F", half_part)])
        else:
            total(whole, dz, cell, part, got)
        if not root:
            returned(key)[0].start()
    for key in RETURNED_BY:
        returned(key)[0].wait_send()


def delay_tables(length):
    indices = np.arange(length, dtype=np.int64)
    angle = (indices[:, None] * indices[None, :] % length) * (2.0 * np.pi / length)
    table = np.concatenate([np.cos(angle), np.sin(angle)], axis=0).astype(np.float32)
    high = table.astype(jnp.bfloat16)
    low = (table - high.astype(np.float32)).astype(jnp.bfloat16)
    return high, low


def body(sky, ker, data, block_tiles, length_bin, wedge_keep):
    per, cells = sky.shape[1], sky.shape[3]
    chans, base = data.shape[3], data.shape[2]
    high, low = delay_tables(chans)
    full = RING * RING
    vmem = pl.BlockSpec(memory_space=pltpu.VMEM)
    hbm = pl.BlockSpec(memory_space=pl.ANY)
    f32, bf16 = jnp.float32, jnp.bfloat16
    out = pl.pallas_call(
        kernel,
        out_shape=jax.ShapeDtypeStruct((2 * per, cells), f32),
        in_specs=[pl.BlockSpec(memory_space=pltpu.SMEM), hbm, hbm, hbm, vmem, hbm, hbm, hbm],
        out_specs=vmem,
        scratch_shapes=[
            pltpu.VMEM((RING, full, ROWS, cells), bf16),
            pltpu.VMEM((cells, 2 * base), bf16),
            pltpu.VMEM((full * ROWS, 2 * base), f32),
            pltpu.VMEM((2, chans, base), f32),
            pltpu.VMEM((chans, base), f32),
            pltpu.VMEM((chans, base), f32),
            pltpu.VMEM((chans, base), f32),
            pltpu.VMEM((chans, base), f32),
            pltpu.VMEM((chans, base), f32),
            pltpu.VMEM((2, chans, base), f32),
            pltpu.VMEM((2 * chans, 2 * base), f32),
            pltpu.VMEM((chans, 2 * base), bf16),
            pltpu.VMEM((chans, 2 * base), bf16),
            pltpu.VMEM((chans, base), f32),
            pltpu.VMEM((2, chans, base), f32),
            pltpu.VMEM((RING, full, ROWS, 2 * base), bf16),
            pltpu.VMEM((RING, full, ROWS, cells), f32),
            pltpu.VMEM((len(HALVES), ROWS, cells // 2), bf16),
            pltpu.VMEM((len(FULLS), ROWS, cells), bf16),
            pltpu.VMEM((RING - 1, ROWS, cells), f32),
            pltpu.VMEM((RING - 1, ROWS, cells), f32),
            pltpu.VMEM((per, 2, cells), bf16),
            pltpu.VMEM((2, base, chans), bf16),
            pltpu.VMEM(wedge_keep.shape, jnp.int32),
            pltpu.VMEM((2 * chans, chans), bf16),
            pltpu.VMEM((2 * chans, chans), bf16),
            pltpu.SemaphoreType.DMA((7,)),
            pltpu.SemaphoreType.DMA((len(SEMAPHORE),)),
            pltpu.SemaphoreType.DMA((len(SEMAPHORE),)),
            pltpu.SemaphoreType.DMA((len(SEMAPHORE),)),
            pltpu.SemaphoreType.DMA((len(GROUPS), 3)),
            pltpu.SemaphoreType.DMA((len(GROUPS), 3)),
        ],
        compiler_params=pltpu.CompilerParams(
            collective_id=0, has_side_effects=True, vmem_limit_bytes=60 * 2**20
        ),
    )(block_tiles, sky[0], ker[0, 0], data[0], length_bin, wedge_keep, high, low)
    return jnp.transpose(out.reshape(2, per, cells), (1, 0, 2))[None]


def solution(mesh):
    finer = Mesh(mesh.devices.reshape(mesh.shape["tile"], RING, RING, RING), AXES)
    return jax.shard_map(
        body,
        mesh=finer,
        in_specs=(
            P("tile", FREQ, None, None),
            P("tile", FREQ, None, None, None),
            P(FREQ, None, None, None),
            P(FREQ, None),
            P(FREQ, None),
            P(),
        ),
        out_specs=P("tile", FREQ, None, None),
        check_vma=False,
    )
```

```python
import functools
import math

import jax
import jax.numpy as jnp
import numpy as np
from jax import lax
from jax.experimental import pallas as pl
from jax.experimental.pallas import tpu as pltpu
from jax.sharding import Mesh
from jax.sharding import PartitionSpec as P

FREQ = ("freq_0", "freq_1", "freq_2")
AXES = ("tile",) + FREQ
RING = 4
ROWS = 16
GATHER_SHAPE = (
    (
        (1, 1, -1, -1, -1, 1, 1, -1),
        (-1, 1, 1, 1, -1, -1, -1, -1),
        (1, 1, 1, -1, 1, -1, -1, 1),
        (1, -1, -1, -1, -1, -1, 1, 1),
    ),
    {(0, "F"): -1, (10, "A"): 1, (10, "B"): -1, (11, "A"): 1, (14, "B"): 1},
)
REDUCE_SHAPE = (
    (
        (1, -1, -1, 1, 1, -1, 1, -1),
        (1, -1, -1, 1, -1, 1, -1, -1),
        (1, 1, 1, 1, 1, 1, -1, 1),
        (-1, -1, -1, -1, -1, -1, -1, -1),
    ),
    {(0, "F"): -1, (10, "A"): 1, (10, "B"): 1, (11, "A"): -1, (14, "B"): 1},
)
SERVE = (
    0, 9, 36, 3, 12, 23, 40, 48, 6, 24, 35, 43, 144, 22, 47, 16, 17, 41, 46, 57, 51, 20, 28, 44,
    -16, 96, 34, 156, 60, -32, 153, 84, 71, 29, 19, 54, 147, 180, 31, 89, 108, 188, -48, 82, 65,
    166, 32, 99, 105, -64, 95, 92, 160, 178, 70, -17, 167, 132, 175, 150, 191, 79, 72, -33, 64,
    94, 185, 68, 140, 83, 190, 161, 88, 112, 118, 168, 163, 80, 184, 176, 137, 77, 113, 136, -18,
    143, 119, 102, 130, -34, 164, 172, 67, 120, 173, 128, 142, 76, 187, -49, 127, 91, 179, -19,
    125, 139, -65, -50, 115, 131, 116, 124, -20, -35, -66, -36, -51, -52, -67, -68,
)
ISSUE = (
    48, 9, 36, 3, 12, 144, 6, 23, 47, 40, 46, 24, 17, 41, 22, 16, 35, 43, 60, 96, 51, 84, 57, 20,
    44, 34, 28, 147, 180, 153, 156, 19, 29, 71, 95, 65, 89, 54, 31, 92, 188, 32, 105, 99, 108,
    132, 178, 82, 160, 166, 70, 72, 64, 191, 150, 167, 94, 88, 83, 68, 185, 161, 184, 168, 190,
    79, 175, 112, 118, 140, 77, 80, 176, 137, 113, 119, 102, 143, 163, 130, 67, 142, 120, 136,
    127, 164, 179, 76, 91, 173, 115, 172, 128, 187, 125, 139, 131, 116, 124,
)
RETURN = (
    116, 125, 124, 115, 130, 68, 131, 128, 136, 112, 139, 137, 113, 172, 118, 80, 83, 76, 127,
    120, 173, 163, 119, 142, 143, 99, 176, 102, 77, 79, 82, 92, 65, 108, 91, 164, 95, 67, 71, 132,
    105, 89, 54, 72, 178, 187, 140, 160, 88, 179, 96, 70, 94, 191, 64, 161, 168, 150, 190, 166,
    57, 167, 185, 175, 32, 184, 51, 60, 84, 188, 147, 153, 180, 34, 31, 43, 156, 20, 44, 19, 47,
    48, 144, 35, 28, 41, 22, 6, 29, 40, 16, 23, 46, 24, 17, 12, 9, 3, 36, 0,
)
GROUPS = (16, 16, 16, 12, 4)


def at(dx, dy):
    return (dx % RING) * RING + dy % RING


def decoded(code):
    return code // 48, code // 3 % 16, "FAB"[code % 3]


def message_tree(shape):
    sides, by_z = shape
    kids = {}

    def edge(parent, axis, step, child):
        if axis == "z" or not (child[0] and child[1:] in by_z):
            kids.setdefault(parent, []).append((axis, step, child))

    for what, side in by_z.items():
        edge((0, *what), "z", -1, (1, *what))
        edge((0, *what), "z", 1, (3, *what))
        edge((2 + side, *what), "z", side, (2, *what))
    for dz in range(RING):
        for turn, part in (("y", "A"), ("x", "B")):
            axis, first = ("x", 0) if part == "A" else ("y", RING)

            def cell(along, across):
                return at(along, across) if axis == "x" else at(across, along)

            side = sides[dz][0]
            for step in (1, -1):
                edge((dz, 0, "F"), axis, step, (dz, cell(-step, 0), "F"))
            edge((dz, cell(-side, 0), "F"), axis, side, (dz, cell(2, 0), "F"))
            for d in range(1, RING):
                for step in (1, -1):
                    edge((dz, cell(d, 0), "F"), turn, step, (dz, cell(d, -step), part))
                side_d = sides[dz][first + d]
                edge((dz, cell(d, -side_d), part), turn, side_d, (dz, cell(d, 2), part))
    return kids


def coded(message):
    return (message[0] * 16 + message[1]) * 3 + "FAB".index(message[2])


def parents(kids):
    return {child: (axis, step) for edges in kids.values() for axis, step, child in edges}


DOWN = message_tree(GATHER_SHAPE)
for edges in DOWN.values():
    edges.sort(key=lambda edge: ISSUE.index(coded(edge[2])))
UP = message_tree(REDUCE_SHAPE)
SERVED_BY = parents(DOWN)
RETURNED_BY = parents(UP)
SEMAPHORE = {message: n for n, message in enumerate(SERVED_BY)}
HALVES = {m: n for n, m in enumerate(m for m in SERVED_BY if m[2] != "F")}
FULLS = {m: n for n, m in enumerate(m for m in SERVED_BY if m[2] == "F" and m[1])}


def kernel(
    bt_ref, sky_ref, ker_ref, data_ref, bins_ref, wedge_ref, thi_ref, tlo_ref, out_ref,
    buf, kc, vp, t1r, hs, hr, tt, tr, vis, spec, vhi, vlo, mask, dat, u, g,
    rs_h, rs_f, zs, zr, raw_sky, raw, wedge, thi, tlo,
    local_sem, send_sem, ag_sem, rs_sem, t_send, t_recv,
):
    tile = lax.axis_index("tile")
    y = lax.axis_index("freq_0")
    z = lax.axis_index("freq_1")
    x = lax.axis_index("freq_2")
    cells = sky_ref.shape[2]
    half = cells // 2
    chans, base = vis.shape[1], vis.shape[2]
    per = chans // RING**3
    core = lax.rem(tile, 2)
    mate = tile + 1 - 2 * core

    def near(axis, step):
        if axis == "x":
            return (tile, y, z, lax.rem(x + step + RING, RING))
        if axis == "y":
            return (tile, lax.rem(y + step + RING, RING), z, x)
        return (tile, y, lax.rem(z + step + RING, RING), x)

    over = lax.rem(tile + 2, 4)
    peers = [near("x", 1), near("x", -1), near("y", 1), near("y", -1)]
    peers += [near("z", 1), near("z", -1)]
    peers += [(t, y, z, x) for t in (mate, over)]

    load_sky = pltpu.make_async_copy(sky_ref, raw_sky, local_sem.at[0])
    load_r = pltpu.make_async_copy(ker_ref.at[0], kc.at[:, 0:base], local_sem.at[1])
    load_i = pltpu.make_async_copy(ker_ref.at[1], kc.at[:, base : 2 * base], local_sem.at[2])
    load_sky.start()
    late = [load_r, load_i]
    for n, (src, dst) in enumerate(
        ((wedge_ref, wedge), (data_ref, raw), (thi_ref, thi), (tlo_ref, tlo))
    ):
        late.append(pltpu.make_async_copy(src, dst, local_sem.at[3 + n]))
    barrier = pltpu.get_barrier_semaphore()
    for peer in peers:
        pl.semaphore_signal(barrier, inc=1, device_id=peer, device_id_type=pl.DeviceIdType.MESH)
    for load in late:
        load.start()
    load_sky.wait()
    buf[0, 0] = jnp.concatenate(
        [raw_sky[:, plane, :].astype(jnp.float32) for plane in range(2)], axis=0
    ).astype(jnp.bfloat16)
    pl.semaphore_wait(barrier, len(peers))

    def part_of(ref, dz, cell, part):
        if part == "F":
            return ref.at[dz, cell]
        lo = 0 if part == "A" else half
        return ref.at[dz, cell, :, lo : lo + half]

    def remote(src, dst, send, recv, peer):
        return pltpu.make_async_remote_copy(
            src_ref=src, dst_ref=dst, send_sem=send, recv_sem=recv,
            device_id=peer, device_id_type=pl.DeviceIdType.MESH,
        )

    weight = bt_ref[0, tile].astype(jnp.float32)

    sent = []

    def gather_serve(key):
        if key in SERVED_BY:
            ref = part_of(buf, *key)
            remote(ref, ref, send_sem.at[0], ag_sem.at[SEMAPHORE[key]], near("x", 1)).wait_recv()
        for axis, step, child in DOWN.get(key, ()):
            copy = remote(
                part_of(buf, *key[:2], child[2]), part_of(buf, *child),
                send_sem.at[SEMAPHORE[child]], ag_sem.at[SEMAPHORE[child]], near(axis, step),
            )
            copy.start()
            sent.append(copy)


    def forward(shards, place):
        count = len(shards)
        value = jnp.concatenate([buf[dz, cell] for dz, cell in shards], axis=0)
        out = jnp.dot(value, kc[...], preferred_element_type=jnp.float32)
        out = out.reshape(count, 2, per, 2 * base)
        real = out[:, 0, :, :base] - out[:, 1, :, base:]
        imag = out[:, 1, :, :base] + out[:, 0, :, base:]
        vp[0, place, :] = (real * weight).reshape(count * per, base)
        vp[1, place, :] = (imag * weight).reshape(count * per, base)

    def t1(n, place):
        return remote(vp.at[1 - core, place], t1r.at[place], t_send.at[n, 0], t_recv.at[n, 0],
                      (mate, y, z, x))

    def t2(n, place):
        return remote(hs.at[place], hr.at[place], t_send.at[n, 1], t_recv.at[n, 1],
                      (over, y, z, x))

    def t3(n, place):
        return remote(tt.at[place], tr.at[place], t_send.at[n, 2], t_recv.at[n, 2],
                      (mate, y, z, x))

    def row_of(dz, cell):
        sx = lax.rem(x + cell // RING, RING)
        sy = lax.rem(y + cell % RING, RING)
        sz = lax.rem(z + dz, RING)
        return pl.multiple_of((sy * RING * RING + sz * RING + sx) * per, per)

    def tile_1(n, shards, place):
        forward(shards, place)
        t1(n, place).start()

    def tile_2(n, shards, place):
        t1(n, place).wait_recv()
        hs[place, :] = vp[core, place, :] + t1r[place, :]
        t2(n, place).start()

    def tile_3(n, shards, place):
        t2(n, place).wait_recv()
        tt[place, :] = hs[place, :] + hr[place, :]
        t3(n, place).start()

    def tile_4(n, shards, place):
        t3(n, place).wait_recv()
        for k, shard in enumerate(shards):
            mine = slice(place.start + k * per, place.start + (k + 1) * per)
            rows = pl.ds(row_of(*shard), per)
            vis[core, rows, :] = tt[mine, :]
            vis[1 - core, rows, :] = tr[mine, :]

    def prepare():
        for load in late:
            load.wait()
        levels = lax.broadcasted_iota(jnp.int32, (wedge.shape[0], base), 0)
        hot = (levels == bins_ref[...]).astype(jnp.bfloat16)
        keep = wedge[...].astype(jnp.float32).T.astype(jnp.bfloat16)
        mask[...] = jnp.dot(keep, hot, preferred_element_type=jnp.float32)
        for plane in range(2):
            dat[plane] = raw[plane].astype(jnp.float32).T

    whole = {}
    for n, code in enumerate(SERVE):
        if code >= 0:
            whole[decoded(code)[:2]] = n
    order = sorted(whole, key=whole.get)
    groups = []
    start = 0
    for n, count in enumerate(GROUPS):
        place = slice(start * per, (start + count) * per)
        groups.append((n, order[start : start + count], place))
        start += count
    for n, code in enumerate(SERVE):
        if code >= 0:
            gather_serve(decoded(code))
        else:
            (tile_1, tile_2, tile_3, tile_4)[-code // 16 - 1](*groups[-code % 16])
        if n == 4:
            prepare()
    for copy in sent:
        copy.wait_send()
    for n, _, place in groups:
        for copy in (t1(n, place), t2(n, place), t3(n, place)):
            copy.wait_send()

    norm = 1.0 / math.sqrt(chans)

    def transform():
        for plane in range(2):
            lanes = slice(plane * base, (plane + 1) * base)
            whole = vis[plane]
            vhi[:, lanes] = whole.astype(jnp.bfloat16)
            vlo[:, lanes] = (whole - vhi[:, lanes].astype(jnp.float32)).astype(jnp.bfloat16)

        spec[...] = (
            jnp.dot(thi[...], vhi[...], preferred_element_type=jnp.float32)
            + jnp.dot(thi[...], vlo[...], preferred_element_type=jnp.float32)
            + jnp.dot(tlo[...], vhi[...], preferred_element_type=jnp.float32)
        )

    cos_rows, sin_rows = slice(0, chans), slice(chans, 2 * chans)
    lane_r, lane_i = slice(0, base), slice(base, 2 * base)
    transform()
    vis[0] = mask[...] * (
        (spec[cos_rows, lane_r] + spec[sin_rows, lane_i]) * norm - dat[0]
    )
    vis[1] = mask[...] * (
        (spec[cos_rows, lane_i] - spec[sin_rows, lane_r]) * norm - dat[1]
    )
    transform()
    vis[0] = (spec[cos_rows, lane_r] - spec[sin_rows, lane_i]) * (norm * weight)
    vis[1] = (spec[cos_rows, lane_i] + spec[sin_rows, lane_r]) * (norm * weight)

    def assemble(dz):
        for cell in range(RING * RING):
            rows = pl.ds(row_of(dz, cell), per)
            ur, ui = vis[0, rows, :], vis[1, rows, :]
            top = jnp.concatenate([ur, ui], axis=1)
            low = jnp.concatenate([ui, -ur], axis=1)
            u[dz, cell] = jnp.concatenate([top, low], axis=0).astype(jnp.bfloat16)

    def backward(dz, part):
        rows = u[dz].reshape(RING * RING * ROWS, 2 * base)
        lanes = slice(0, half) if part == "A" else slice(half, cells)
        value = lax.dot_general(
            rows, kc[lanes, :], (((1,), (1,)), ((), ())), preferred_element_type=jnp.float32
        )
        g[dz, :, :, lanes] = value.reshape(RING * RING, ROWS, half)

    width = 1024

    def total(dst, dz, cell, part, terms):
        start = half if part == "B" else 0
        stop = half if part == "A" else cells

        def step_of(n):
            lanes = pl.ds(pl.multiple_of(start + n * width, width), width)
            value = g[dz, cell, :, lanes]
            for ref, kind in terms:
                shift = half if kind == "B" else 0
                own = pl.ds(pl.multiple_of(start - shift + n * width, width), width)
                value = value + ref[:, own].astype(jnp.float32)
            if dst is out_ref:
                for plane in range(2):
                    dst[:, plane, lanes] = value[plane * per : (plane + 1) * per]
            else:
                dst[:, lanes] = value.astype(dst.dtype)

        pl.loop(0, (stop - start) // width)(step_of)

    def returned(key):
        dz, cell, part = key
        axis, step = RETURNED_BY[key]
        if cell == 0 and dz and axis == "z":
            src, dst = zs.at[dz - 1], zr.at[dz - 1]
        else:
            src = part_of(buf, *key)
            dst = rs_f.at[FULLS[key]] if part == "F" else rs_h.at[HALVES[key]]
        n = SEMAPHORE[key]
        return remote(src, dst, send_sem.at[n], rs_sem.at[n], near(axis, -step)), src, dst

    ready = set()
    for code in RETURN:
        key = decoded(code)
        dz, cell, part = key
        root = key not in RETURNED_BY
        for half_part in "AB" if part == "F" else part:
            if (dz, half_part) not in ready:
                if not ready & {(dz, "A"), (dz, "B")}:
                    assemble(dz)
                ready.add((dz, half_part))
                backward(dz, half_part)
        got = []
        for _, _, child in UP.get(key, ()):
            copy, _, dst = returned(child)
            copy.wait_recv()
            got.append((dst, child[2]))
        whole = out_ref if root else zs.at[dz - 1] if cell == 0 else buf.at[dz, cell]
        kinds = {kind for _, kind in got}
        if part == "F" and kinds - {"F"}:
            for half_part in "AB":
                total(whole, dz, cell, half_part, [t for t in got if t[1] in ("F", half_part)])
        else:
            total(whole, dz, cell, part, got)
        if not root:
            returned(key)[0].start()
    for key in RETURNED_BY:
        returned(key)[0].wait_send()


def delay_tables(length):
    indices = np.arange(length, dtype=np.int64)
    angle = (indices[:, None] * indices[None, :] % length) * (2.0 * np.pi / length)
    table = np.concatenate([np.cos(angle), np.sin(angle)], axis=0).astype(np.float32)
    high = table.astype(jnp.bfloat16)
    low = (table - high.astype(np.float32)).astype(jnp.bfloat16)
    return high, low


def body(sky, ker, data, block_tiles, length_bin, wedge_keep):
    per, cells = sky.shape[1], sky.shape[3]
    chans, base = data.shape[3], data.shape[2]
    high, low = delay_tables(chans)
    full = RING * RING
    vmem = pl.BlockSpec(memory_space=pltpu.VMEM)
    hbm = pl.BlockSpec(memory_space=pl.ANY)
    f32, bf16 = jnp.float32, jnp.bfloat16
    out = pl.pallas_call(
        kernel,
        out_shape=jax.ShapeDtypeStruct((per, 2, cells), f32),
        in_specs=[pl.BlockSpec(memory_space=pltpu.SMEM), hbm, hbm, hbm, vmem, hbm, hbm, hbm],
        out_specs=vmem,
        scratch_shapes=[
            pltpu.VMEM((RING, full, ROWS, cells), bf16),
            pltpu.VMEM((cells, 2 * base), bf16),
            pltpu.VMEM((2, chans, base), f32),
            pltpu.VMEM((chans, base), f32),
            pltpu.VMEM((chans, base), f32),
            pltpu.VMEM((chans, base), f32),
            pltpu.VMEM((chans, base), f32),
            pltpu.VMEM((chans, base), f32),
            pltpu.VMEM((2, chans, base), f32),
            pltpu.VMEM((2 * chans, 2 * base), f32),
            pltpu.VMEM((chans, 2 * base), bf16),
            pltpu.VMEM((chans, 2 * base), bf16),
            pltpu.VMEM((chans, base), f32),
            pltpu.VMEM((2, chans, base), f32),
            pltpu.VMEM((RING, full, ROWS, 2 * base), bf16),
            pltpu.VMEM((RING, full, ROWS, cells), f32),
            pltpu.VMEM((len(HALVES), ROWS, cells // 2), bf16),
            pltpu.VMEM((len(FULLS), ROWS, cells), bf16),
            pltpu.VMEM((RING - 1, ROWS, cells), f32),
            pltpu.VMEM((RING - 1, ROWS, cells), f32),
            pltpu.VMEM((per, 2, cells), bf16),
            pltpu.VMEM((2, base, chans), bf16),
            pltpu.VMEM(wedge_keep.shape, jnp.int32),
            pltpu.VMEM((2 * chans, chans), bf16),
            pltpu.VMEM((2 * chans, chans), bf16),
            pltpu.SemaphoreType.DMA((7,)),
            pltpu.SemaphoreType.DMA((len(SEMAPHORE),)),
            pltpu.SemaphoreType.DMA((len(SEMAPHORE),)),
            pltpu.SemaphoreType.DMA((len(SEMAPHORE),)),
            pltpu.SemaphoreType.DMA((len(GROUPS), 3)),
            pltpu.SemaphoreType.DMA((len(GROUPS), 3)),
        ],
        compiler_params=pltpu.CompilerParams(
            collective_id=0, has_side_effects=True, vmem_limit_bytes=60 * 2**20
        ),
    )(block_tiles, sky[0], ker[0, 0], data[0], length_bin, wedge_keep, high, low)
    return out[None]


def solution(mesh):
    finer = Mesh(mesh.devices.reshape(mesh.shape["tile"], RING, RING, RING), AXES)
    return jax.shard_map(
        body,
        mesh=finer,
        in_specs=(
            P("tile", FREQ, None, None),
            P("tile", FREQ, None, None, None),
            P(FREQ, None, None, None),
            P(FREQ, None),
            P(FREQ, None),
            P(),
        ),
        out_specs=P("tile", FREQ, None, None),
        check_vma=False,
    )
```
